256 devices in a mesh: layer: 4 (over y), front: 64 (over z, x, core).
Axes of the slice: x: 4, y: 4, z: 8, core: 2. Of those that a mesh axis runs over, the one named last changes fastest.
Arguments:
- right_sides: float32 [4, 2, 4, 8192], P('layer', None, None, 'front'), may hold values from -6 to 6
- leaf_inverse: bfloat16 [4, 2, 8192, 128], P('layer', None, 'front'), may hold values from -0.375 to 0.375
- couple_above: bfloat16 [4, 2, 8192, 128], P('layer', None, 'front'), may hold values from -0.1875 to 0.1875
- couple_below: bfloat16 [4, 2, 8192, 128], P('layer', None, 'front'), may hold values from -0.1875 to 0.1875
- sep_gather: bfloat16 [4, 2, 5120, 8192], P('layer', None, None, 'front'), may hold values from -0.046875 to 0.046875
- sep_inverse: bfloat16 [4, 2, 5120, 5120], P('layer', None, 'front'), may hold values from -0.0625 to 0.0625
- sep_spread: bfloat16 [4, 2, 8192, 5120], P('layer', None, 'front'), may hold values from -0.0625 to 0.0625
- panel_owner: int32 [4, 64], P('layer'), may hold values from 0 to 63, each once within a row
Outputs:
- solution: float32 [4, 2, 4, 8192], P('layer', None, None, 'front')
The draws below stay inside these ranges and needn't reach their ends.
Inputs may be any that keep to these rules, and one draw needn't show every extreme that they name: Each row of panel_owner names every slot 0 to 63 once.
All inputs are finite; a program needn't handle non-finite values.
Results may differ from the reference program's by a relative error of at most 0.023.
Values may be sent and summed in bfloat16 or wider, within the bound.
A program may use at most 128 MiB of HBM per device.

```python
import jax
import jax.numpy as jnp

CELLS_DEV = 128
SEP = 5120
RHS = 4
LAYERS = 4
CELLS = 8192
N_LAYER = 4
N_FRONT = 64


def block_scale(rng, extent, split, least, top_value):
    level, own = 1.0, jax.random.fold_in(rng, 6)
    for axis_at, shards_of in split:
        steps = jnp.exp(jax.random.uniform(jax.random.fold_in(own, axis_at), (shards_of,), jnp.float32, least / len(split), top_value / len(split)))
        level = level * jnp.repeat(steps, extent[axis_at] // shards_of).reshape([-1 if axis == axis_at else 1 for axis in range(len(extent))])
    return level


def centred(key, shape, width, most, split=(), dtype=jnp.bfloat16):
    drawn = width * jax.random.normal(key, shape, jnp.float32)
    if split:
        drawn = drawn * block_scale(key, shape, split, -0.22, 0.18)
    return jnp.clip(drawn, -most, most).astype(dtype)


def setup_inputs(seed: int = 0) -> dict:
    key_list = jax.random.split(jax.random.key(seed), 9)
    return {
        "right_sides": centred(key_list[0], (LAYERS, 2, RHS, CELLS), 1.0, 6.0, ((0, 4), (3, 64)), jnp.float32),
        "leaf_inverse": centred(key_list[1], (LAYERS, 2, CELLS, CELLS_DEV), (2 * CELLS_DEV) ** -0.5, 0.375, ((0, 4), (2, 64))),
        "couple_above": centred(key_list[2], (LAYERS, 2, CELLS, CELLS_DEV), (8 * CELLS_DEV) ** -0.5, 0.1875, ((0, 4), (2, 64))),
        "couple_below": centred(key_list[3], (LAYERS, 2, CELLS, CELLS_DEV), (8 * CELLS_DEV) ** -0.5, 0.1875, ((0, 4), (2, 64))),
        "sep_gather": centred(key_list[4], (LAYERS, 2, SEP, CELLS), (2 * CELLS) ** -0.5, 0.046875, ((0, 4), (3, 64))),
        "sep_inverse": centred(key_list[5], (LAYERS, 2, SEP, SEP), (2 * SEP) ** -0.5, 0.0625, ((0, 4), (2, 64))),
        "sep_spread": centred(key_list[6], (LAYERS, 2, CELLS, SEP), (2 * SEP) ** -0.5, 0.0625, ((0, 4), (2, 64))),
        "panel_owner": jax.vmap(lambda own: jax.random.permutation(own, N_FRONT))(jax.random.split(key_list[7], LAYERS)).reshape((LAYERS, N_FRONT)).astype(jnp.int32),
    }


def dense_apply(matrix, vector):
    def single(left, right):
        return jnp.dot(right, left.T, preferred_element_type=jnp.float32)
    real_part = single(matrix[0], vector[0]) - single(matrix[1], vector[1])
    imag_part = single(matrix[0], vector[1]) + single(matrix[1], vector[0])
    return jnp.stack([real_part, imag_part])


def block_apply(matrix, vector):
    blocks = matrix.astype(jnp.float32).reshape(2, -1, CELLS_DEV, CELLS_DEV)
    pieces = vector.astype(jnp.float32).reshape(2, RHS, -1, CELLS_DEV)

    def single(left, right):
        return jnp.einsum('nmk,rnk->rnm', left, right)
    real_part = single(blocks[0], pieces[0]) - single(blocks[1], pieces[1])
    imag_part = single(blocks[0], pieces[1]) + single(blocks[1], pieces[0])
    return jnp.stack([real_part, imag_part]).reshape(2, RHS, -1)


def layer_solve(source, leaf, gather_map, sep_matrix, spread):
    leaf_values = block_apply(leaf, source.astype(jnp.bfloat16))
    sep_sums = dense_apply(gather_map, leaf_values.astype(jnp.bfloat16))
    sep_values = dense_apply(sep_matrix, sep_sums.astype(jnp.bfloat16)).astype(jnp.bfloat16)
    return leaf_values - dense_apply(spread, sep_values)


def reference(right_sides, leaf_inverse, couple_above, couple_below, sep_gather, sep_inverse, sep_spread, panel_owner):
    ordered = []
    for level in range(N_LAYER):
        panels = sep_inverse[level].reshape(2, N_FRONT, SEP // N_FRONT, SEP)
        ordered.append(jnp.take(panels, panel_owner[level].astype(jnp.int32), axis=1).reshape(2, SEP, SEP))

    def solve(level, source):
        return layer_solve(source, leaf_inverse[level], sep_gather[level], ordered[level], sep_spread[level])

    forward = [solve(0, right_sides[0])]
    for level in range(1, N_LAYER):
        coupled = block_apply(couple_above[level], forward[level - 1].astype(jnp.bfloat16))
        forward.append(solve(level, right_sides[level] - coupled))
    solved = [None] * N_LAYER
    solved[N_LAYER - 1] = forward[N_LAYER - 1]
    for level in range(N_LAYER - 2, -1, -1):
        coupled = block_apply(couple_below[level], solved[level + 1].astype(jnp.bfloat16))
        solved[level] = forward[level] - solve(level, coupled)
    return jnp.stack(solved)
```

```python
import functools

import jax
import jax.numpy as jnp
from jax import lax
from jax.experimental import pallas as pl
from jax.experimental.pallas import tpu as pltpu
from jax.sharding import PartitionSpec as P

MESH = pl.DeviceIdType.MESH
F32 = jnp.float32
BF16 = jnp.bfloat16
ROWS = 8
GROUP = 8


def widen(v):
    turned = pltpu.roll(v, 4, 0)
    row = lax.broadcasted_iota(jnp.int32, v.shape, 0)
    turned = jnp.where(row < 4, -turned, turned)
    return jnp.concatenate([v, turned], axis=1).astype(BF16)


def times(wide, matrix):
    return lax.dot_general(wide, matrix, (((1,), (1,)), ((), ())), preferred_element_type=F32)


def kernel(
    depth, cells, sep, panel,
    owner, rs, leaf_h, above_h, below_h, gather_h, inv_h, spread_h,
    out,
    leaf, above, below, gath, qmat, spread,
    abuf, arecv, bbuf, brecv, cbuf, crecv, dbuf, vall, natural, fbuf, frecv, held,
    load_sem, q_send, q_recv, send_sem, recv_sem, f_send, f_recv,
):
    ly = lax.axis_index("layer")
    me = lax.axis_index("front")
    z, r = me // GROUP, lax.rem(me, GROUP)
    block = sep // GROUP

    def row_peer(k):
        return (ly, z * GROUP + lax.rem(r + k, GROUP))

    def col_peer(k):
        return (ly, lax.rem(z + k, GROUP) * GROUP + r)

    def load(src, dst, at):
        copy = pltpu.make_async_copy(src, dst, load_sem.at[at])
        copy.start()
        return copy

    loads = []
    n = 0
    for src, dst, width in (
        (leaf_h, leaf, cells), (gather_h, gath, cells), (spread_h, spread, sep),
        (above_h, above, cells), (below_h, below, cells),
    ):
        pair = []
        for part in range(2):
            pair.append(load(src.at[part], dst.at[:, pl.ds(part * width, width)], n))
            n += 1
        loads.append(pair)
    own_q = []
    for part in range(2):
        own_q.append(load(
            inv_h.at[part, :, pl.ds(pl.multiple_of(r * block, 128), block)],
            qmat.at[r, pl.ds(0, panel), pl.ds(part * block, block)], n))
        n += 1

    barrier = pltpu.get_barrier_semaphore()
    for k in range(1, GROUP):
        pl.semaphore_signal(barrier, inc=1, device_id=row_peer(k), device_id_type=MESH)
        pl.semaphore_signal(barrier, inc=1, device_id=col_peer(k), device_id_type=MESH)

    @pl.when(ly > 0)
    def _():
        pl.semaphore_signal(barrier, inc=1, device_id=(ly - 1, me), device_id_type=MESH)

    @pl.when(ly < depth - 1)
    def _():
        pl.semaphore_signal(barrier, inc=1, device_id=(ly + 1, me), device_id_type=MESH)

    ends = (ly == 0).astype(jnp.int32) + (ly == depth - 1).astype(jnp.int32)
    pl.semaphore_wait(barrier, 2 * (GROUP - 1) + 2 - ends)

    q_copies = []
    for k in range(1, GROUP):
        to = lax.rem(r + k, GROUP)
        for part in range(2):
            copy = pltpu.make_async_remote_copy(
                src_ref=inv_h.at[part, :, pl.ds(pl.multiple_of(to * block, 128), block)],
                dst_ref=qmat.at[r, pl.ds(0, panel), pl.ds(part * block, block)],
                send_sem=q_send.at[k - 1, part],
                recv_sem=q_recv.at[k - 1, part],
                device_id=row_peer(k), device_id_type=MESH)
            copy.start()
            q_copies.append(copy)
    qmat[:, panel:, :] = jnp.zeros((GROUP, 128 - panel, 2 * block), BF16)

    order = (4, 3, 5, 2, 6, 1, 7)

    def wait_all(ref, sem):
        pltpu.make_async_copy(ref, ref, sem).wait()

    def exchange(s, phase, peer, src, recv, local):
        copies = []
        for k in order:
            copy = pltpu.make_async_remote_copy(
                src_ref=src(k), dst_ref=recv.at[s, k - 1],
                send_sem=send_sem.at[s, phase], recv_sem=recv_sem.at[s, phase],
                device_id=peer(k), device_id_type=MESH)
            copy.start()
        wait_all(recv.at[s], recv_sem.at[s, phase])
        total = local
        for k in range(GROUP - 1):
            total = total + recv[s, k].astype(F32)
        return total

    def solve(s, source):
        leaf_values = times(widen(source), leaf[...])
        wide = widen(leaf_values)
        for j in range(GROUP):
            abuf[s, j] = times(wide, gath[pl.ds(j * block, block), :]).astype(BF16)
        mine = exchange(s, 0, row_peer, lambda k: abuf.at[s, lax.rem(r + k, GROUP)], arecv, abuf[s, r].astype(F32))
        bbuf[s] = mine.astype(BF16)
        sums = exchange(s, 1, col_peer, lambda k: bbuf.at[s], brecv, mine)
        wide = widen(sums)
        for c in range(GROUP):
            cbuf[s, c] = times(wide, qmat[c]).astype(BF16)
        values = exchange(s, 2, row_peer, lambda k: cbuf.at[s], crecv, cbuf[s].astype(F32))
        dbuf[s] = values.astype(BF16)
        for k in order:
            pltpu.make_async_remote_copy(
                src_ref=dbuf.at[s], dst_ref=vall.at[s, z],
                send_sem=send_sem.at[s, 3], recv_sem=recv_sem.at[s, 3],
                device_id=col_peer(k), device_id_type=MESH).start()
        vall[s, z] = dbuf[s]
        wait_all(vall.at[s, pl.ds(0, GROUP - 1)], recv_sem.at[s, 3])
        lane = lax.broadcasted_iota(jnp.int32, (ROWS, 128), 1)
        tile, at = None, 0
        for p in range(sep // panel):
            slot = owner[p]
            chunk = vall[s, slot // GROUP, lax.rem(slot, GROUP)].astype(F32)
            start = p * panel - at * 128
            moved = pltpu.roll(chunk, start, 1) if start else chunk
            tile = moved if tile is None else jnp.where(lane >= start, moved, tile)
            if start + panel >= 128:
                natural[:, at * 128:(at + 1) * 128] = tile
                at += 1
                tile = moved if start + panel > 128 else None
        wide = widen(natural[...])
        return leaf_values - times(wide, spread[...])

    def hop(s, to, value):
        fbuf[s] = value.astype(BF16)
        return pltpu.make_async_remote_copy(
            src_ref=fbuf.at[s], dst_ref=frecv.at[s], send_sem=f_send.at[s], recv_sem=f_recv.at[s],
            device_id=(to, me), device_id_type=MESH)

    def sent(s):
        for phase, buf in ((0, arecv), (1, brecv), (2, crecv)):
            wait_all(buf.at[s], send_sem.at[s, phase])
        wait_all(vall.at[s, pl.ds(0, GROUP - 1)], send_sem.at[s, 3])

    for pair in loads:
        for copy in pair:
            copy.wait()

    @pl.when(ly == 0)
    def _():
        held[0] = rs[...]

    @pl.when(ly > 0)
    def _():
        wait_all(frecv.at[0], f_recv.at[0])
        held[0] = rs[...] - times(widen(frecv[0].astype(F32)), above[...])

    for copy in own_q:
        copy.wait()
    for copy in q_copies:
        copy.wait_recv()
    forward = solve(0, held[0])
    held[1] = forward

    @pl.when(ly < depth - 1)
    def _():
        hop(0, ly + 1, held[1]).start()

    @pl.when(ly == depth - 1)
    def _():
        out[...] = held[1]

    @pl.when(ly < depth - 1)
    def _():
        wait_all(frecv.at[1], f_recv.at[1])
        solved = held[1] - solve(1, times(widen(frecv[1].astype(F32)), below[...]))
        out[...] = solved
        wait_all(frecv.at[0], f_send.at[0])

    @pl.when(ly > 0)
    def _():
        copy = hop(1, ly - 1, out[...])
        copy.start()
        copy.wait_send()

    for copy in q_copies:
        copy.wait_send()
    sent(0)

    @pl.when(ly < depth - 1)
    def _():
        sent(1)


def local(right_sides, leaf, above, below, gather, inverse, spread, owner):
    depth = lax.axis_size("layer")
    _, _, count, cells = right_sides.shape
    panel, sep = inverse.shape[2], inverse.shape[3]
    block = sep // GROUP
    vmem = pl.BlockSpec(memory_space=pltpu.VMEM)
    hbm = pl.BlockSpec(memory_space=pl.ANY)
    dma = pltpu.SemaphoreType.DMA
    out = pl.pallas_call(
        functools.partial(kernel, depth, cells, sep, panel),
        out_shape=jax.ShapeDtypeStruct((ROWS, cells), F32),
        in_specs=[pl.BlockSpec(memory_space=pltpu.SMEM), vmem] + [hbm] * 6,
        out_specs=vmem,
        scratch_shapes=[
            pltpu.VMEM((cells, 2 * cells), BF16),
            pltpu.VMEM((cells, 2 * cells), BF16),
            pltpu.VMEM((cells, 2 * cells), BF16),
            pltpu.VMEM((sep, 2 * cells), BF16),
            pltpu.VMEM((GROUP, 128, 2 * block), BF16),
            pltpu.VMEM((cells, 2 * sep), BF16),
            pltpu.VMEM((2, GROUP, ROWS, block), BF16),
            pltpu.VMEM((2, GROUP - 1, ROWS, block), BF16),
            pltpu.VMEM((2, ROWS, block), BF16),
            pltpu.VMEM((2, GROUP - 1, ROWS, block), BF16),
            pltpu.VMEM((2, GROUP, ROWS, 128), BF16),
            pltpu.VMEM((2, GROUP - 1, GROUP, ROWS, 128), BF16),
            pltpu.VMEM((2, GROUP, ROWS, 128), BF16),
            pltpu.VMEM((2, GROUP, GROUP, ROWS, 128), BF16),
            pltpu.VMEM((ROWS, sep), F32),
            pltpu.VMEM((2, ROWS, cells), BF16),
            pltpu.VMEM((2, ROWS, cells), BF16),
            pltpu.VMEM((2, ROWS, cells), F32),
            dma((12,)),
            dma((GROUP - 1, 2)),
            dma((GROUP - 1, 2)),
            dma((2, 4)),
            dma((2, 4)),
            dma((2,)),
            dma((2,)),
        ],
        compiler_params=pltpu.CompilerParams(
            collective_id=0, has_side_effects=True, vmem_limit_bytes=40 * 2**20),
        name="sweep",
    )(owner[0], right_sides.reshape(ROWS, cells), leaf[0], above[0], below[0], gather[0], inverse[0], spread[0])
    return out.reshape(1, 2, count, cells)


def solution(mesh):
    return jax.shard_map(
        local,
        mesh=mesh,
        in_specs=(
            P("layer", None, None, "front"),
            P("layer", None, "front", None),
            P("layer", None, "front", None),
            P("layer", None, "front", None),
            P("layer", None, None, "front"),
            P("layer", None, "front", None),
            P("layer", None, "front", None),
            P("layer", None),
        ),
        out_specs=P("layer", None, None, "front"),
        check_vma=False,
    )
```

```python
import functools

import jax
import jax.numpy as jnp
from jax import lax
from jax.experimental import pallas as pl
from jax.experimental.pallas import tpu as pltpu
from jax.sharding import PartitionSpec as P

MESH = pl.DeviceIdType.MESH
F32 = jnp.float32
BF16 = jnp.bfloat16
ROWS = 8
GROUP = 8
ORDER = (4, 3, 5, 2, 6, 1, 7)
PLAIN = 2


def widen(v):
    turned = pltpu.roll(v, 4, 0)
    row = lax.broadcasted_iota(jnp.int32, v.shape, 0)
    turned = jnp.where(row < 4, -turned, turned)
    return jnp.concatenate([v, turned], axis=1).astype(BF16)


def dot_nt(a, b):
    return lax.dot_general(a, b, (((1,), (1,)), ((), ())), preferred_element_type=F32)


def dot_nn(a, b):
    return lax.dot_general(a, b, (((1,), (0,)), ((), ())), preferred_element_type=F32)


def expand(stack, n):
    top, low = stack[:n], stack[n:]
    return jnp.concatenate(
        [jnp.concatenate([top, -low], axis=1), jnp.concatenate([low, top], axis=1)], axis=0).astype(BF16)


def kernel(
    depth, cells, sep, panel,
    slots, rs, leaf_h, above_h, below_h, gather_h, inv_h, spread_h,
    out,
    leaf, above, below, gath, qmat, pnat, leaf_t, la_t, lb_t, xa, xb, qt, pt, pts, po,
    abuf, arecv, bbuf, brecv, cbuf, crecv, dbuf, vall, fbuf, fone, obuf, orecv, frecv,
    const, lead, held, prod,
    load_sem, q_send, q_recv, p_send, p_recv, send_sem, recv_sem, one_send, one_recv,
    y_send, y_recv, o_send, o_recv,
):
    ly = lax.axis_index("layer")
    me = lax.axis_index("front")
    z, r = me // GROUP, lax.rem(me, GROUP)
    block = sep // GROUP

    def row_peer(k):
        return (ly, z * GROUP + lax.rem(r + k, GROUP))

    def col_peer(k):
        return (ly, lax.rem(z + k, GROUP) * GROUP + r)

    def wait_all(ref, sem):
        pltpu.make_async_copy(ref, ref, sem).wait()

    loads = {}
    n = 0
    for name, src, dst in (("leaf", leaf_h, leaf), ("gath", gather_h, gath), ("below", below_h, below), ("above", above_h, above)):
        loads[name] = []
        for part in range(2):
            copy = pltpu.make_async_copy(src.at[part], dst.at[:, pl.ds(part * cells, cells)], load_sem.at[n])
            copy.start()
            loads[name].append(copy)
            n += 1
    loads["spread"] = [pltpu.make_async_copy(spread_h, pnat, load_sem.at[n])]
    loads["spread"][0].start()
    n += 1
    loads["own"] = []
    for part in range(2):
        copy = pltpu.make_async_copy(
            inv_h.at[part, :, pl.ds(pl.multiple_of(r * block, 128), block)],
            qmat.at[pl.ds(pl.multiple_of(r * panel, 16), panel), pl.ds(part * block, block)], load_sem.at[n])
        copy.start()
        loads["own"].append(copy)
        n += 1

    def arrive(name):
        for copy in loads[name]:
            copy.wait()

    barrier = pltpu.get_barrier_semaphore()
    for k in range(1, GROUP):
        pl.semaphore_signal(barrier, inc=1, device_id=row_peer(k), device_id_type=MESH)
        pl.semaphore_signal(barrier, inc=1, device_id=col_peer(k), device_id_type=MESH)

    @pl.when(ly > 0)
    def _():
        for k in range(GROUP):
            pl.semaphore_signal(barrier, inc=1, device_id=(ly - 1, k * GROUP + r), device_id_type=MESH)

    @pl.when(ly < depth - 1)
    def _():
        for k in range(GROUP):
            pl.semaphore_signal(barrier, inc=1, device_id=(ly + 1, k * GROUP + r), device_id_type=MESH)

    arrive("leaf")
    arrive("gath")
    first = dot_nt(widen(rs[...]), leaf[...])
    lead[0] = first
    wide = widen(first)
    for j in range(GROUP):
        const[j] = dot_nt(wide, gath[pl.ds(j * block, block), :])

    ends = (ly == 0).astype(jnp.int32) + (ly == depth - 1).astype(jnp.int32)
    pl.semaphore_wait(barrier, 2 * (GROUP - 1) + GROUP * (2 - ends))

    def send_a(s, k):
        pltpu.make_async_remote_copy(
            src_ref=abuf.at[s, lax.rem(r + k, GROUP)], dst_ref=arecv.at[s, k - 1],
            send_sem=send_sem.at[s, 0], recv_sem=recv_sem.at[s, 0],
            device_id=row_peer(k), device_id_type=MESH).start()

    @pl.when(ly == 0)
    def _():
        for j in range(GROUP):
            abuf[0, j] = const[j].astype(BF16)
        for k in ORDER:
            send_a(0, k)

    for k in ORDER:
        to = lax.rem(r + k, GROUP)
        for part in range(2):
            pltpu.make_async_remote_copy(
                src_ref=inv_h.at[part, :, pl.ds(pl.multiple_of(to * block, 128), block)],
                dst_ref=qmat.at[pl.ds(pl.multiple_of(r * panel, 16), panel), pl.ds(part * block, block)],
                send_sem=q_send, recv_sem=q_recv,
                device_id=row_peer(k), device_id_type=MESH).start()

    arrive("below")
    arrive("above")
    leaf_t[...] = leaf[...].T
    leaf_stack = leaf_t[...]
    for coupling, folded, product in ((below, lb_t, xb), (above, la_t, xa)):
        left = expand(coupling[...].T.astype(F32), cells)
        stack = dot_nn(left, leaf_stack)
        folded[...] = stack.astype(BF16)
        left = expand(stack, cells)
        for j in range(GROUP):
            product[:, j * block:(j + 1) * block] = dot_nt(left, gath[pl.ds(j * block, block), :]).astype(BF16)

    arrive("spread")
    for part in range(2):
        for j in range(GROUP):
            turned = pnat[part, :, j * block:(j + 1) * block].T
            per = block // panel
            pt[part, pl.ds(j * per, per)] = turned.reshape(per, panel, cells)

    for slot in range(sep // panel):
        at = slots[slot]
        for part in range(2):
            pts[part, slot * panel:(slot + 1) * panel, :] = pt[part, at]

    def share_spread():
        for k in ORDER:
            to = lax.rem(z + k, GROUP)
            for part in range(2):
                pltpu.make_async_remote_copy(
                    src_ref=pts.at[part, pl.ds(pl.multiple_of(to * block, 128), block)],
                    dst_ref=po.at[pl.ds(part * block, block), pl.ds(pl.multiple_of(z * cells, 128), cells)],
                    send_sem=p_send, recv_sem=p_recv, device_id=col_peer(k), device_id_type=MESH).start()
        for part in range(2):
            po[pl.ds(part * block, block), pl.ds(pl.multiple_of(z * cells, 128), cells)] = (
                pts[part, pl.ds(pl.multiple_of(z * block, 128), block), :])

    p_bytes = po.at[:, pl.ds(0, (GROUP - 1) * cells)]
    q_bytes = qmat.at[pl.ds(0, (GROUP - 1) * panel), :]

    @pl.when(ly >= PLAIN)
    def _():
        share_spread()

    @pl.when(ly > 0)
    def _():
        @pl.when(ly <= PLAIN)
        def _():
            wait_all(fone, one_recv)
            held[0] = fone[...].astype(F32)

        @pl.when(ly > PLAIN)
        def _():
            wait_all(frecv.at[0], y_recv.at[0])
            total = frecv[0, 0].astype(F32)
            for k in range(1, GROUP):
                total = total + frecv[0, k].astype(F32)
            held[0] = total

        wide = widen(held[0])
        for k in ORDER + (0,):
            j = lax.rem(r + k, GROUP)
            cols = pl.ds(pl.multiple_of(j * block, 128), block)
            abuf[0, j] = (const[j] - dot_nn(wide, xa[:, cols])).astype(BF16)
            if k:
                send_a(0, k)
        lead[0] = lead[0] - dot_nn(wide, la_t[...])

    def middle(s):
        wait_all(arecv.at[s], recv_sem.at[s, 0])
        total = abuf[s, r].astype(F32)
        for k in range(GROUP - 1):
            total = total + arecv[s, k].astype(F32)
        bbuf[s] = total.astype(BF16)
        for k in ORDER:
            pltpu.make_async_remote_copy(
                src_ref=bbuf.at[s], dst_ref=brecv.at[s, k - 1],
                send_sem=send_sem.at[s, 1], recv_sem=recv_sem.at[s, 1],
                device_id=col_peer(k), device_id_type=MESH).start()
        if s == 0:
            arrive("own")
            wait_all(q_bytes, q_recv)
            qt[...] = qmat[...].T
        wait_all(brecv.at[s], recv_sem.at[s, 1])
        for k in range(GROUP - 1):
            total = total + brecv[s, k].astype(F32)
        mine = dot_nn(widen(total), qt[...])
        cbuf[s] = mine.astype(BF16)
        for k in ORDER:
            pltpu.make_async_remote_copy(
                src_ref=cbuf.at[s], dst_ref=crecv.at[s, k - 1],
                send_sem=send_sem.at[s, 2], recv_sem=recv_sem.at[s, 2],
                device_id=row_peer(k), device_id_type=MESH).start()
        wait_all(crecv.at[s], recv_sem.at[s, 2])
        for k in range(GROUP - 1):
            mine = mine + crecv[s, k].astype(F32)
        return mine

    def spread_out(s, values, own, sign, to, lane):
        shares = sign * dot_nn(widen(values), po[...])
        for j in range(GROUP):
            prod[j] = shares[:, j * cells:(j + 1) * cells]
            obuf[s, j] = shares[:, j * cells:(j + 1) * cells].astype(BF16)
        total = own + prod[z]
        obuf[s, z] = total.astype(BF16)

        @pl.when(to >= 0)
        def _():
            for k in ORDER + (0,):
                j = lax.rem(z + k, GROUP)
                pltpu.make_async_remote_copy(
                    src_ref=obuf.at[s, j], dst_ref=frecv.at[lane, k],
                    send_sem=y_send.at[s], recv_sem=y_recv.at[lane],
                    device_id=(to, j * GROUP + r), device_id_type=MESH).start()

        for k in ORDER:
            j = lax.rem(z + k, GROUP)
            pltpu.make_async_remote_copy(
                src_ref=obuf.at[s, j], dst_ref=orecv.at[s, k - 1],
                send_sem=o_send.at[s], recv_sem=o_recv.at[s],
                device_id=(ly, j * GROUP + r), device_id_type=MESH).start()
        wait_all(orecv.at[s], o_recv.at[s])
        for k in range(GROUP - 1):
            total = total + orecv[s, k].astype(F32)
        return total

    values = middle(0)
    dbuf[...] = values

    @pl.when(ly < PLAIN)
    def _():
        cbuf[2] = dbuf[...].astype(BF16)
        for k in ORDER:
            pltpu.make_async_remote_copy(
                src_ref=cbuf.at[2], dst_ref=vall.at[z], send_sem=send_sem.at[0, 3], recv_sem=recv_sem.at[0, 3],
                device_id=col_peer(k), device_id_type=MESH).start()
        vall[z] = cbuf[2]
        wait_all(vall.at[pl.ds(0, GROUP - 1)], recv_sem.at[0, 3])
        gathered = jnp.concatenate([vall[k].astype(F32) for k in range(GROUP)], axis=1)
        wide = widen(gathered)
        forward = lead[0] - dot_nn(wide[:, :sep], pts[0]) - dot_nn(wide[:, sep:], pts[1])
        held[1] = forward
        fbuf[...] = forward.astype(BF16)
        pltpu.make_async_remote_copy(
            src_ref=fbuf, dst_ref=fone, send_sem=one_send, recv_sem=one_recv,
            device_id=(ly + 1, me), device_id_type=MESH).start()
        share_spread()

    @pl.when(ly >= PLAIN)
    def _():
        wait_all(p_bytes, p_recv)
        last = ly == depth - 1
        held[1] = spread_out(0, dbuf[...], lead[0], -1.0, jnp.where(last, ly - 1, ly + 1), last.astype(jnp.int32))

    @pl.when(ly == depth - 1)
    def _():
        out[...] = held[1]

    @pl.when(ly < depth - 1)
    def _():
        wait_all(frecv.at[1], y_recv.at[1])
        total = frecv[1, 0].astype(F32)
        for k in range(1, GROUP):
            total = total + frecv[1, k].astype(F32)
        wide = widen(total)
        for k in ORDER + (0,):
            j = lax.rem(r + k, GROUP)
            cols = pl.ds(pl.multiple_of(j * block, 128), block)
            abuf[1, j] = dot_nn(wide, xb[:, cols]).astype(BF16)
            if k:
                send_a(1, k)
        held[1] = held[1] - dot_nn(wide, lb_t[...])
        values = middle(1)

        @pl.when(ly < PLAIN)
        def _():
            wait_all(p_bytes, p_recv)

        out[...] = spread_out(1, values, held[1], 1.0, ly - 1, 1)

    wait_all(q_bytes, q_send)
    wait_all(p_bytes, p_send)

    def sent(s):
        for phase, buf in ((0, arecv), (1, brecv), (2, crecv)):
            wait_all(buf.at[s], send_sem.at[s, phase])

    sent(0)

    @pl.when(ly < PLAIN)
    def _():
        wait_all(vall.at[pl.ds(0, GROUP - 1)], send_sem.at[0, 3])
        wait_all(fone, one_send)

    @pl.when(ly >= PLAIN)
    def _():
        wait_all(frecv.at[0], y_send.at[0])
        wait_all(orecv.at[0], o_send.at[0])

    @pl.when(ly < depth - 1)
    def _():
        sent(1)
        wait_all(orecv.at[1], o_send.at[1])

        @pl.when(ly > 0)
        def _():
            wait_all(frecv.at[1], y_send.at[1])


def local(right_sides, leaf, above, below, gather, inverse, spread, owner):
    depth = lax.axis_size("layer")
    _, _, count, cells = right_sides.shape
    panel, sep = inverse.shape[2], inverse.shape[3]
    block = sep // GROUP
    vmem = pl.BlockSpec(memory_space=pltpu.VMEM)
    hbm = pl.BlockSpec(memory_space=pl.ANY)
    dma = pltpu.SemaphoreType.DMA
    slot = jnp.arange(sep // panel, dtype=jnp.int32)
    slots = jnp.sum(jnp.where(owner[0][:, None] == slot[None, :], slot[:, None], 0), axis=0)
    V = pltpu.VMEM
    out = pl.pallas_call(
        functools.partial(kernel, depth, cells, sep, panel),
        out_shape=jax.ShapeDtypeStruct((ROWS, cells), F32),
        in_specs=[pl.BlockSpec(memory_space=pltpu.SMEM), vmem] + [hbm] * 6,
        out_specs=vmem,
        scratch_shapes=[
            V((cells, 2 * cells), BF16),
            V((cells, 2 * cells), BF16),
            V((cells, 2 * cells), BF16),
            V((sep, 2 * cells), BF16),
            V((block, 2 * block), BF16),
            V((2, cells, sep), BF16),
            V((2 * cells, cells), BF16),
            V((2 * cells, cells), BF16),
            V((2 * cells, cells), BF16),
            V((2 * cells, sep), BF16),
            V((2 * cells, sep), BF16),
            V((2 * block, block), BF16),
            V((2, sep // panel, panel, cells), BF16),
            V((2, sep, cells), BF16),
            V((2 * block, GROUP * cells), BF16),
            V((2, GROUP, ROWS, block), BF16),
            V((2, GROUP - 1, ROWS, block), BF16),
            V((2, ROWS, block), BF16),
            V((2, GROUP - 1, ROWS, block), BF16),
            V((3, ROWS, block), BF16),
            V((2, GROUP - 1, ROWS, block), BF16),
            V((ROWS, block), F32),
            V((GROUP, ROWS, block), BF16),
            V((ROWS, cells), BF16),
            V((ROWS, cells), BF16),
            V((2, GROUP, ROWS, cells), BF16),
            V((2, GROUP - 1, ROWS, cells), BF16),
            V((2, GROUP, ROWS, cells), BF16),
            V((GROUP, ROWS, block), F32),
            V((1, ROWS, cells), F32),
            V((2, ROWS, cells), F32),
            V((GROUP, ROWS, cells), F32),
            dma((11,)),
            dma, dma, dma, dma,
            dma((2, 4)), dma((2, 4)),
            dma, dma,
            dma((2,)), dma((2,)), dma((2,)), dma((2,)),
        ],
        compiler_params=pltpu.CompilerParams(
            collective_id=0, has_side_effects=True, vmem_limit_bytes=60 * 2**20),
        name="sweep",
    )(slots, right_sides.reshape(ROWS, cells), leaf[0], above[0], below[0], gather[0], inverse[0], spread[0])
    return out.reshape(1, 2, count, cells)


def solution(mesh):
    return jax.shard_map(
        local,
        mesh=mesh,
        in_specs=(
            P("layer", None, None, "front"),
            P("layer", None, "front", None),
            P("layer", None, "front", None),
            P("layer", None, "front", None),
            P("layer", None, None, "front"),
            P("layer", None, "front", None),
            P("layer", None, "front", None),
            P("layer", None),
        ),
        out_specs=P("layer", None, None, "front"),
        check_vma=False,
    )
```

```python
import functools

import jax
import jax.numpy as jnp
from jax import lax
from jax.experimental import pallas as pl
from jax.experimental.pallas import tpu as pltpu
from jax.sharding import PartitionSpec as P

MESH = pl.DeviceIdType.MESH
F32 = jnp.float32
BF16 = jnp.bfloat16
ROWS = 8
GROUP = 8
ORDER = (4, 3, 5, 2, 6, 1, 7)
PLAIN = 2


def widen(v):
    turned = pltpu.roll(v, 4, 0)
    row = lax.broadcasted_iota(jnp.int32, v.shape, 0)
    turned = jnp.where(row < 4, -turned, turned)
    return jnp.concatenate([v, turned], axis=1).astype(BF16)


def dot_nt(a, b):
    return lax.dot_general(a, b, (((1,), (1,)), ((), ())), preferred_element_type=F32)


def dot_nn(a, b):
    return lax.dot_general(a, b, (((1,), (0,)), ((), ())), preferred_element_type=F32)


def expand(stack, n):
    top, low = stack[:n], stack[n:]
    return jnp.concatenate(
        [jnp.concatenate([top, -low], axis=1), jnp.concatenate([low, top], axis=1)], axis=0).astype(BF16)


def kernel(
    depth, cells, sep, panel,
    slots, rs, leaf_h, above_h, below_h, gather_h, inv_h, spread_h,
    out,
    leaf, above, below, gath, qmat, pnat, leaf_t, la_t, lb_t, xa, xb, qt, pt, pts, po,
    abuf, arecv, bbuf, brecv, cbuf, crecv, dbuf, vall, fbuf, fone, obuf, orecv, frecv,
    const, lead, held, prod, qown, sall, vown,
    load_sem, q_send, q_recv, p_send, p_recv, send_sem, recv_sem, one_send, one_recv,
    y_send, y_recv, o_send, o_recv, v_send, v_recv,
):
    ly = lax.axis_index("layer")
    me = lax.axis_index("front")
    z, r = me // GROUP, lax.rem(me, GROUP)
    block = sep // GROUP

    def row_peer(k):
        return (ly, z * GROUP + lax.rem(r + k, GROUP))

    def col_peer(k):
        return (ly, lax.rem(z + k, GROUP) * GROUP + r)

    def wait_all(ref, sem):
        pltpu.make_async_copy(ref, ref, sem).wait()

    p_bytes = po.at[:, pl.ds(0, (GROUP - 1) * cells)]
    q_bytes = qmat.at[pl.ds(0, (GROUP - 1) * panel), :]

    loads = {}
    n = 0
    for name, src, dst in (("leaf", leaf_h, leaf), ("gath", gather_h, gath), ("below", below_h, below), ("above", above_h, above)):
        loads[name] = []
        for part in range(2):
            copy = pltpu.make_async_copy(src.at[part], dst.at[:, pl.ds(part * cells, cells)], load_sem.at[n])
            copy.start()
            loads[name].append(copy)
            n += 1
    loads["spread"] = [pltpu.make_async_copy(spread_h, pnat, load_sem.at[n])]
    loads["spread"][0].start()
    n += 1
    loads["own"] = []
    for part in range(2):
        copy = pltpu.make_async_copy(
            inv_h.at[part, :, pl.ds(pl.multiple_of(z * block, 128), block)],
            qmat.at[pl.ds(pl.multiple_of(z * panel, 16), panel), pl.ds(part * block, block)], load_sem.at[n])
        copy.start()
        loads["own"].append(copy)
        n += 1
    loads["panel"] = []
    for part in range(2):
        copy = pltpu.make_async_copy(inv_h.at[part], qown.at[:, pl.ds(part * sep, sep)], load_sem.at[n])
        copy.start()
        loads["panel"].append(copy)
        n += 1

    def arrive(name):
        for copy in loads[name]:
            copy.wait()

    barrier = pltpu.get_barrier_semaphore()
    for k in range(1, GROUP):
        pl.semaphore_signal(barrier, inc=1, device_id=row_peer(k), device_id_type=MESH)
        pl.semaphore_signal(barrier, inc=1, device_id=col_peer(k), device_id_type=MESH)

    @pl.when(ly > 0)
    def _():
        for k in range(GROUP):
            pl.semaphore_signal(barrier, inc=1, device_id=(ly - 1, z * GROUP + k), device_id_type=MESH)

    @pl.when(ly < depth - 1)
    def _():
        for k in range(GROUP):
            pl.semaphore_signal(barrier, inc=1, device_id=(ly + 1, z * GROUP + k), device_id_type=MESH)

    arrive("leaf")
    arrive("gath")
    first = dot_nt(widen(rs[...]), leaf[...])
    lead[0] = first
    wide = widen(first)
    for j in range(GROUP):
        const[j] = dot_nt(wide, gath[pl.ds(j * block, block), :])

    ends = (ly == 0).astype(jnp.int32) + (ly == depth - 1).astype(jnp.int32)
    pl.semaphore_wait(barrier, 2 * (GROUP - 1) + GROUP * (2 - ends))

    def send_a(s, k, at, peer):
        pltpu.make_async_remote_copy(
            src_ref=abuf.at[s, lax.rem(at + k, GROUP)], dst_ref=arecv.at[s, k - 1],
            send_sem=send_sem.at[s, 0], recv_sem=recv_sem.at[s, 0],
            device_id=peer(k), device_id_type=MESH).start()

    @pl.when(ly == 0)
    def _():
        for j in range(GROUP):
            abuf[0, j] = const[j].astype(BF16)
        for k in ORDER:
            send_a(0, k, r, row_peer)

    def share_inverse():
        for k in ORDER:
            to = lax.rem(z + k, GROUP)
            for part in range(2):
                pltpu.make_async_remote_copy(
                    src_ref=inv_h.at[part, :, pl.ds(pl.multiple_of(to * block, 128), block)],
                    dst_ref=qmat.at[pl.ds(pl.multiple_of(z * panel, 16), panel), pl.ds(part * block, block)],
                    send_sem=q_send, recv_sem=q_recv,
                    device_id=col_peer(k), device_id_type=MESH).start()

    def take_inverse():
        arrive("own")
        wait_all(q_bytes, q_recv)
        qt[...] = qmat[...].T

    def fold(pairs):
        leaf_t[...] = leaf[...].T
        leaf_stack = leaf_t[...]
        for coupling, folded, product in pairs:
            left = expand(coupling[...].T.astype(F32), cells)
            stack = dot_nn(left, leaf_stack)
            folded[...] = stack.astype(BF16)
            left = expand(stack, cells)
            for j in range(GROUP):
                product[:, j * block:(j + 1) * block] = dot_nt(left, gath[pl.ds(j * block, block), :]).astype(BF16)

    def turn_spread():
        for part in range(2):
            for j in range(GROUP):
                turned = pnat[part, :, j * block:(j + 1) * block].T
                per = block // panel
                pt[part, pl.ds(j * per, per)] = turned.reshape(per, panel, cells)
        for slot in range(sep // panel):
            at = slots[slot % GROUP * GROUP + slot // GROUP]
            for part in range(2):
                pts[part, slot * panel:(slot + 1) * panel, :] = pt[part, at]

    def share_spread():
        for k in ORDER:
            to = lax.rem(r + k, GROUP)
            for part in range(2):
                pltpu.make_async_remote_copy(
                    src_ref=pts.at[part, pl.ds(pl.multiple_of(to * block, 128), block)],
                    dst_ref=po.at[pl.ds(part * block, block), pl.ds(pl.multiple_of(r * cells, 128), cells)],
                    send_sem=p_send, recv_sem=p_recv, device_id=row_peer(k), device_id_type=MESH).start()
        for part in range(2):
            po[pl.ds(part * block, block), pl.ds(pl.multiple_of(r * cells, 128), cells)] = (
                pts[part, pl.ds(pl.multiple_of(r * block, 128), block), :])

    arrive("below")
    arrive("above")
    arrive("spread")

    @pl.when(ly >= PLAIN)
    def _():
        share_inverse()

    turn_spread()

    @pl.when(ly >= PLAIN)
    def _():
        share_spread()

    @pl.when(ly > 0)
    def _():
        fold(((above, la_t, xa), (below, lb_t, xb)))

    @pl.when(ly > 0)
    def _():
        @pl.when(ly <= PLAIN)
        def _():
            wait_all(fone, one_recv)
            held[0] = fone[...].astype(F32)

        @pl.when(ly > PLAIN)
        def _():
            wait_all(frecv.at[0], y_recv.at[0])
            total = frecv[0, 0].astype(F32)
            for k in range(1, GROUP):
                total = total + frecv[0, k].astype(F32)
            held[0] = total

        wide = widen(held[0])

        def send_all(at, peer):
            for k in ORDER + (0,):
                j = lax.rem(at + k, GROUP)
                cols = pl.ds(pl.multiple_of(j * block, 128), block)
                abuf[0, j] = (const[j] - dot_nn(wide, xa[:, cols])).astype(BF16)
                if k:
                    send_a(0, k, at, peer)

        @pl.when(ly < PLAIN)
        def _():
            send_all(r, row_peer)

        @pl.when(ly >= PLAIN)
        def _():
            send_all(z, col_peer)

        lead[0] = lead[0] - dot_nn(wide, la_t[...])

    @pl.when(ly >= PLAIN)
    def _():
        take_inverse()

    def sum_block(s, at, peer):
        wait_all(arecv.at[s], recv_sem.at[s, 0])
        total = abuf[s, at].astype(F32)
        for k in range(GROUP - 1):
            total = total + arecv[s, k].astype(F32)
        bbuf[s] = total.astype(BF16)
        for k in ORDER:
            pltpu.make_async_remote_copy(
                src_ref=bbuf.at[s], dst_ref=brecv.at[s, k - 1],
                send_sem=send_sem.at[s, 1], recv_sem=recv_sem.at[s, 1],
                device_id=peer(k), device_id_type=MESH).start()
        wait_all(brecv.at[s], recv_sem.at[s, 1])
        for k in range(GROUP - 1):
            total = total + brecv[s, k].astype(F32)
        return total

    def value_block(s, total):
        mine = dot_nn(widen(total), qt[...])
        cbuf[s] = mine.astype(BF16)
        for k in ORDER:
            pltpu.make_async_remote_copy(
                src_ref=cbuf.at[s], dst_ref=crecv.at[s, k - 1],
                send_sem=send_sem.at[s, 2], recv_sem=recv_sem.at[s, 2],
                device_id=col_peer(k), device_id_type=MESH).start()
        wait_all(crecv.at[s], recv_sem.at[s, 2])
        for k in range(GROUP - 1):
            mine = mine + crecv[s, k].astype(F32)
        return mine

    def panel_block(total):
        sall[r] = total.astype(BF16)
        for k in ORDER:
            pltpu.make_async_remote_copy(
                src_ref=sall.at[r], dst_ref=sall.at[r], send_sem=send_sem.at[0, 2], recv_sem=recv_sem.at[0, 2],
                device_id=row_peer(k), device_id_type=MESH).start()
        wait_all(sall.at[pl.ds(0, GROUP - 1)], recv_sem.at[0, 2])
        wide = widen(jnp.concatenate([sall[k].astype(F32) for k in range(GROUP)], axis=1))
        mine = dot_nt(wide, qown[...])
        vown[z] = jnp.concatenate([mine, jnp.zeros((ROWS, 128 - panel), F32)], axis=1).astype(BF16)
        for k in ORDER:
            pltpu.make_async_remote_copy(
                src_ref=vown.at[z], dst_ref=vown.at[z], send_sem=v_send, recv_sem=v_recv,
                device_id=col_peer(k), device_id_type=MESH).start()
        wait_all(vown.at[pl.ds(0, GROUP - 1)], v_recv)
        return jnp.concatenate([vown[k].astype(F32)[:, :panel] for k in range(GROUP)], axis=1)

    def spread_out(s, values, own, sign, to, lane):
        shares = sign * dot_nn(widen(values), po[...])
        for j in range(GROUP):
            prod[j] = shares[:, j * cells:(j + 1) * cells]
            obuf[s, j] = shares[:, j * cells:(j + 1) * cells].astype(BF16)
        total = own + prod[r]
        obuf[s, r] = total.astype(BF16)

        @pl.when(to >= 0)
        def _():
            for k in ORDER + (0,):
                j = lax.rem(r + k, GROUP)
                pltpu.make_async_remote_copy(
                    src_ref=obuf.at[s, j], dst_ref=frecv.at[lane, k],
                    send_sem=y_send.at[s], recv_sem=y_recv.at[lane],
                    device_id=(to, z * GROUP + j), device_id_type=MESH).start()

        for k in ORDER:
            j = lax.rem(r + k, GROUP)
            pltpu.make_async_remote_copy(
                src_ref=obuf.at[s, j], dst_ref=orecv.at[s, k - 1],
                send_sem=o_send.at[s], recv_sem=o_recv.at[s],
                device_id=(ly, z * GROUP + j), device_id_type=MESH).start()
        wait_all(orecv.at[s], o_recv.at[s])
        for k in range(GROUP - 1):
            total = total + orecv[s, k].astype(F32)
        return total

    def second(k):
        across, along = row_peer(k)[1], col_peer(k)[1]
        return (ly, jnp.where(ly < PLAIN, along, across))

    sums = sum_block(0, jnp.where(ly < PLAIN, r, z), second)

    @pl.when(ly < PLAIN)
    def _():
        arrive("panel")
        dbuf[...] = panel_block(sums)

    @pl.when(ly >= PLAIN)
    def _():
        dbuf[...] = value_block(0, sums)

    @pl.when(ly < PLAIN)
    def _():
        cbuf[2] = dbuf[...].astype(BF16)
        for k in ORDER:
            pltpu.make_async_remote_copy(
                src_ref=cbuf.at[2], dst_ref=vall.at[r], send_sem=send_sem.at[0, 3], recv_sem=recv_sem.at[0, 3],
                device_id=row_peer(k), device_id_type=MESH).start()
        vall[r] = cbuf[2]
        wait_all(vall.at[pl.ds(0, GROUP - 1)], recv_sem.at[0, 3])
        gathered = jnp.concatenate([vall[k].astype(F32) for k in range(GROUP)], axis=1)
        wide = widen(gathered)
        forward = lead[0] - dot_nn(wide[:, :sep], pts[0]) - dot_nn(wide[:, sep:], pts[1])
        held[1] = forward
        fbuf[...] = forward.astype(BF16)
        pltpu.make_async_remote_copy(
            src_ref=fbuf, dst_ref=fone, send_sem=one_send, recv_sem=one_recv,
            device_id=(ly + 1, me), device_id_type=MESH).start()
        share_inverse()
        share_spread()

        @pl.when(ly == 0)
        def _():
            fold(((below, lb_t, xb),))

        take_inverse()

    @pl.when(ly >= PLAIN)
    def _():
        wait_all(p_bytes, p_recv)
        last = ly == depth - 1
        held[1] = spread_out(0, dbuf[...], lead[0], -1.0, jnp.where(last, ly - 1, ly + 1), last.astype(jnp.int32))

    @pl.when(ly == depth - 1)
    def _():
        out[...] = held[1]

    @pl.when(ly < depth - 1)
    def _():
        wait_all(frecv.at[1], y_recv.at[1])
        total = frecv[1, 0].astype(F32)
        for k in range(1, GROUP):
            total = total + frecv[1, k].astype(F32)
        wide = widen(total)
        for k in ORDER + (0,):
            j = lax.rem(z + k, GROUP)
            cols = pl.ds(pl.multiple_of(j * block, 128), block)
            abuf[1, j] = dot_nn(wide, xb[:, cols]).astype(BF16)
            if k:
                send_a(1, k, z, col_peer)
        held[1] = held[1] - dot_nn(wide, lb_t[...])
        values = value_block(1, sum_block(1, z, row_peer))

        @pl.when(ly < PLAIN)
        def _():
            wait_all(p_bytes, p_recv)

        out[...] = spread_out(1, values, held[1], 1.0, ly - 1, 1)

    wait_all(q_bytes, q_send)
    wait_all(p_bytes, p_send)

    def sent(s):
        for phase, buf in ((0, arecv), (1, brecv), (2, crecv)):
            wait_all(buf.at[s], send_sem.at[s, phase])

    sent(0)

    @pl.when(ly < PLAIN)
    def _():
        wait_all(vown.at[pl.ds(0, GROUP - 1)], v_send)

    @pl.when(ly >= PLAIN)
    def _():
        arrive("panel")

    @pl.when(ly < PLAIN)
    def _():
        wait_all(vall.at[pl.ds(0, GROUP - 1)], send_sem.at[0, 3])
        wait_all(fone, one_send)

    @pl.when(ly >= PLAIN)
    def _():
        wait_all(frecv.at[0], y_send.at[0])
        wait_all(orecv.at[0], o_send.at[0])

    @pl.when(ly < depth - 1)
    def _():
        sent(1)
        wait_all(orecv.at[1], o_send.at[1])

        @pl.when(ly > 0)
        def _():
            wait_all(frecv.at[1], y_send.at[1])


def local(right_sides, leaf, above, below, gather, inverse, spread, owner):
    depth = lax.axis_size("layer")
    _, _, count, cells = right_sides.shape
    panel, sep = inverse.shape[2], inverse.shape[3]
    block = sep // GROUP
    vmem = pl.BlockSpec(memory_space=pltpu.VMEM)
    hbm = pl.BlockSpec(memory_space=pl.ANY)
    dma = pltpu.SemaphoreType.DMA
    slot = jnp.arange(sep // panel, dtype=jnp.int32)
    slots = jnp.sum(jnp.where(owner[0][:, None] == slot[None, :], slot[:, None], 0), axis=0)
    V = pltpu.VMEM
    out = pl.pallas_call(
        functools.partial(kernel, depth, cells, sep, panel),
        out_shape=jax.ShapeDtypeStruct((ROWS, cells), F32),
        in_specs=[pl.BlockSpec(memory_space=pltpu.SMEM), vmem] + [hbm] * 6,
        out_specs=vmem,
        scratch_shapes=[
            V((cells, 2 * cells), BF16),
            V((cells, 2 * cells), BF16),
            V((cells, 2 * cells), BF16),
            V((sep, 2 * cells), BF16),
            V((block, 2 * block), BF16),
            V((2, cells, sep), BF16),
            V((2 * cells, cells), BF16),
            V((2 * cells, cells), BF16),
            V((2 * cells, cells), BF16),
            V((2 * cells, sep), BF16),
            V((2 * cells, sep), BF16),
            V((2 * block, block), BF16),
            V((2, sep // panel, panel, cells), BF16),
            V((2, sep, cells), BF16),
            V((2 * block, GROUP * cells), BF16),
            V((2, GROUP, ROWS, block), BF16),
            V((2, GROUP - 1, ROWS, block), BF16),
            V((2, ROWS, block), BF16),
            V((2, GROUP - 1, ROWS, block), BF16),
            V((3, ROWS, block), BF16),
            V((2, GROUP - 1, ROWS, block), BF16),
            V((ROWS, block), F32),
            V((GROUP, ROWS, block), BF16),
            V((ROWS, cells), BF16),
            V((ROWS, cells), BF16),
            V((2, GROUP, ROWS, cells), BF16),
            V((2, GROUP - 1, ROWS, cells), BF16),
            V((2, GROUP, ROWS, cells), BF16),
            V((GROUP, ROWS, block), F32),
            V((1, ROWS, cells), F32),
            V((2, ROWS, cells), F32),
            V((GROUP, ROWS, cells), F32),
            V((panel, 2 * sep), BF16),
            V((GROUP, ROWS, block), BF16),
            V((GROUP, ROWS, 128), BF16),
            dma((13,)),
            dma, dma, dma, dma,
            dma((2, 4)), dma((2, 4)),
            dma, dma,
            dma((2,)), dma((2,)), dma((2,)), dma((2,)), dma, dma,
        ],
        compiler_params=pltpu.CompilerParams(
            collective_id=0, has_side_effects=True, vmem_limit_bytes=60 * 2**20),
        name="sweep",
    )(slots, right_sides.reshape(ROWS, cells), leaf[0], above[0], below[0], gather[0], inverse[0], spread[0])
    return out.reshape(1, 2, count, cells)


def solution(mesh):
    return jax.shard_map(
        local,
        mesh=mesh,
        in_specs=(
            P("layer", None, None, "front"),
            P("layer", None, "front", None),
            P("layer", None, "front", None),
            P("layer", None, "front", None),
            P("layer", None, None, "front"),
            P("layer", None, "front", None),
            P("layer", None, "front", None),
            P("layer", None),
        ),
        out_specs=P("layer", None, None, "front"),
        check_vma=False,
    )
```

```python
import functools

import jax
import jax.numpy as jnp
from jax import lax
from jax.experimental import pallas as pl
from jax.experimental.pallas import tpu as pltpu
from jax.sharding import PartitionSpec as P

MESH = pl.DeviceIdType.MESH
F32 = jnp.float32
BF16 = jnp.bfloat16
ROWS = 8
GROUP = 8
ORDER = (4, 3, 5, 2, 6, 1, 7)


def widen(v):
    turned = pltpu.roll(v, 4, 0)
    row = lax.broadcasted_iota(jnp.int32, v.shape, 0)
    turned = jnp.where(row < 4, -turned, turned)
    return jnp.concatenate([v, turned], axis=1).astype(BF16)


def dot_nt(a, b):
    return lax.dot_general(a, b, (((1,), (1,)), ((), ())), preferred_element_type=F32)


def dot_nn(a, b):
    return lax.dot_general(a, b, (((1,), (0,)), ((), ())), preferred_element_type=F32)


def expand(stack, n):
    top, low = stack[:n], stack[n:]
    return jnp.concatenate(
        [jnp.concatenate([top, -low], axis=1), jnp.concatenate([low, top], axis=1)], axis=0).astype(BF16)


def kernel(
    depth, cells, sep, panel,
    slots, rs, leaf_h, above_h, below_h, gather_h, inv_h, spread_h,
    out,
    leaf, above, below, gath, qmat, pnat, leaf_t, la_t, lb_t, xa, xb, xo, qt, pt, pts, po, qown,
    abuf, arecv, bbuf, brecv, cbuf, crecv, crow, sall, vown, vall, fbuf, fone, obuf, orecv, frecv, frow,
    const, lead, held, prod,
    load_sem, send_sem, recv_sem, bulk_send, bulk_recv, one_send, one_recv,
    y_send, y_recv, w_recv, o_send, o_recv, v_send, v_recv,
):
    ly = lax.axis_index("layer")
    me = lax.axis_index("front")
    z, r = me // GROUP, lax.rem(me, GROUP)
    block = sep // GROUP
    Q_AT, P_AT, X_AT, C_AT = range(4)

    def row_peer(k):
        return (ly, z * GROUP + lax.rem(r + k, GROUP))

    def col_peer(k):
        return (ly, lax.rem(z + k, GROUP) * GROUP + r)

    def wait_all(ref, sem):
        pltpu.make_async_copy(ref, ref, sem).wait()

    def send(src, dst, send_at, recv_at, to):
        pltpu.make_async_remote_copy(
            src_ref=src, dst_ref=dst, send_sem=send_at, recv_sem=recv_at, device_id=to, device_id_type=MESH).start()

    def part_of(index, size):
        return pl.ds(pl.multiple_of(index * size, 128 if size % 128 == 0 else 16), size)

    bulk = (
        qmat.at[pl.ds(0, (GROUP - 1) * panel), :],
        po.at[:, pl.ds(0, (GROUP - 1) * cells)],
        xo.at[pl.ds(0, (GROUP - 1) * 2 * cells), :],
        crow,
    )

    loads = {}
    n = 0
    for name, src, dst in (("leaf", leaf_h, leaf), ("gath", gather_h, gath), ("below", below_h, below), ("above", above_h, above)):
        loads[name] = []
        for part in range(2):
            copy = pltpu.make_async_copy(src.at[part], dst.at[:, pl.ds(part * cells, cells)], load_sem.at[n])
            copy.start()
            loads[name].append(copy)
            n += 1
    loads["spread"] = [pltpu.make_async_copy(spread_h, pnat, load_sem.at[n])]
    loads["spread"][0].start()
    n += 1
    even = lax.rem(ly, 2) == 0
    place = jnp.where(even, z, r)
    loads["own"], loads["panel"] = [], []
    for part in range(2):
        loads["own"].append(pltpu.make_async_copy(
            inv_h.at[part, :, part_of(place, block)],
            qmat.at[part_of(place, panel), pl.ds(part * block, block)], load_sem.at[n]))
        loads["panel"].append(pltpu.make_async_copy(inv_h.at[part], qown.at[:, pl.ds(part * sep, sep)], load_sem.at[n + 1]))
        n += 2
    for copy in loads["own"]:
        copy.start()

    @pl.when(ly == 0)
    def _():
        for copy in loads["panel"]:
            copy.start()

    def arrive(name):
        for copy in loads[name]:
            copy.wait()

    barrier = pltpu.get_barrier_semaphore()

    def greet(to):
        pl.semaphore_signal(barrier, inc=1, device_id=to, device_id_type=MESH)

    for k in range(1, GROUP):
        greet(row_peer(k))
        greet(col_peer(k))
    for low, along_row, along_col in ((0, False, True), (1, True, False), (2, True, True)):
        for mine, other in ((low, low + 1), (low + 1, low)):
            @pl.when(ly == mine)
            def _(other=other, along_row=along_row, along_col=along_col):
                greet((other, me))
                for k in range(1, GROUP):
                    if along_row:
                        greet((other, row_peer(k)[1]))
                    if along_col:
                        greet((other, col_peer(k)[1]))

    arrive("leaf")
    arrive("gath")
    first = dot_nt(widen(rs[...]), leaf[...])
    lead[0] = first
    wide = widen(first)
    for j in range(GROUP):
        const[j] = dot_nt(wide, gath[pl.ds(j * block, block), :])

    greeted = (GROUP, 2 * GROUP, 3 * GROUP - 1, 2 * GROUP - 1)
    extra = jnp.where(ly == 0, greeted[0], jnp.where(ly == 1, greeted[1], jnp.where(ly == 2, greeted[2], greeted[3])))
    pl.semaphore_wait(barrier, 2 * (GROUP - 1) + extra)

    def scatter(s, at, peer, term):
        for k in ORDER + (0,):
            j = lax.rem(at + k, GROUP)
            abuf[s, j] = term(j).astype(BF16)
            if k:
                send(abuf.at[s, j], arecv.at[s, k - 1], send_sem.at[s, 0], recv_sem.at[s, 0], peer(k))

    def scattered(s, at):
        wait_all(arecv.at[s], recv_sem.at[s, 0])
        total = abuf[s, at].astype(F32)
        for k in range(GROUP - 1):
            total = total + arecv[s, k].astype(F32)
        return total

    def add_up(s, phase, mine, buf, recv, peer):
        buf[s] = mine.astype(BF16)
        for k in ORDER:
            send(buf.at[s], recv.at[s, k - 1], send_sem.at[s, phase], recv_sem.at[s, phase], peer(k))
        wait_all(recv.at[s], recv_sem.at[s, phase])
        for k in range(GROUP - 1):
            mine = mine + recv[s, k].astype(F32)
        return mine

    def values_of(s, partial, sums_peer, values_peer):
        sums = add_up(s, 1, partial, bbuf, brecv, sums_peer)
        return add_up(s, 2, dot_nn(widen(sums), qt[...]), cbuf, crecv, values_peer)

    def gather_into(ref, at, peer, send_at, recv_at):
        for k in ORDER:
            send(ref.at[at], ref.at[at], send_at, recv_at, peer(k))
        wait_all(ref.at[pl.ds(0, GROUP - 1)], recv_at)

    def share_inverse(at, peer):
        for k in ORDER:
            for part in range(2):
                send(inv_h.at[part, :, part_of(lax.rem(at + k, GROUP), block)],
                     qmat.at[part_of(at, panel), pl.ds(part * block, block)],
                     bulk_send.at[Q_AT], bulk_recv.at[Q_AT], peer(k))

    def take_inverse():
        arrive("own")
        wait_all(bulk[Q_AT], bulk_recv.at[Q_AT])
        qt[...] = qmat[...].T

    def share_spread(at, peer):
        for k in ORDER:
            for part in range(2):
                send(pts.at[part, part_of(lax.rem(at + k, GROUP), block)],
                     po.at[pl.ds(part * block, block), part_of(at, cells)],
                     bulk_send.at[P_AT], bulk_recv.at[P_AT], peer(k))
        for part in range(2):
            po[pl.ds(part * block, block), part_of(at, cells)] = pts[part, part_of(at, block), :]

    def take_spread():
        wait_all(bulk[P_AT], bulk_recv.at[P_AT])

    def share_product(product):
        for k in ORDER:
            send(product.at[:, part_of(lax.rem(r + k, GROUP), block)], xo.at[part_of(r, 2 * cells), :],
                 bulk_send.at[X_AT], bulk_recv.at[X_AT], row_peer(k))
        xo[part_of(r, 2 * cells), :] = product[:, part_of(r, block)]

    def take_product():
        wait_all(bulk[X_AT], bulk_recv.at[X_AT])

    def fold(pairs):
        leaf_t[...] = leaf[...].T
        leaf_stack = leaf_t[...]
        for coupling, folded, product in pairs:
            left = expand(coupling[...].T.astype(F32), cells)
            stack = dot_nn(left, leaf_stack)
            folded[...] = stack.astype(BF16)
            left = expand(stack, cells)
            for j in range(GROUP):
                product[:, j * block:(j + 1) * block] = dot_nt(left, gath[pl.ds(j * block, block), :]).astype(BF16)

    def turn_spread():
        for part in range(2):
            for j in range(GROUP):
                turned = pnat[part, :, j * block:(j + 1) * block].T
                per = block // panel
                pt[part, pl.ds(j * per, per)] = turned.reshape(per, panel, cells)

    def order_spread(order):
        for place, slot in enumerate(order):
            at = slots[slot]
            for part in range(2):
                pts[part, place * panel:(place + 1) * panel, :] = pt[part, at]

    by_z = range(GROUP * GROUP)
    by_r = [zz * GROUP + rr for rr in range(GROUP) for zz in range(GROUP)]

    def plain_end(values, at, peer):
        vall[at] = values.astype(BF16)
        gather_into(vall, at, peer, send_sem.at[0, 3], recv_sem.at[0, 3])
        wide = widen(jnp.concatenate([vall[k].astype(F32) for k in range(GROUP)], axis=1))
        forward = lead[0] - dot_nn(wide[:, :sep], pts[0]) - dot_nn(wide[:, sep:], pts[1])
        held[...] = forward
        fbuf[...] = forward.astype(BF16)
        send(fbuf, fone, one_send, one_recv, (ly + 1, me))

    def spread_out(s, values, own, sign, at, peer, to, whole):
        shares = sign * dot_nn(widen(values), po[...])
        for j in range(GROUP):
            prod[j] = shares[:, j * cells:(j + 1) * cells]
            obuf[s, j] = shares[:, j * cells:(j + 1) * cells].astype(BF16)
        total = own + prod[at]
        obuf[s, at] = total.astype(BF16)
        if to is not None:
            for k in ORDER + (0,):
                if whole:
                    send(obuf.at[s], frow.at[k], y_send, w_recv, (to, peer(k)[1]))
                else:
                    send(obuf.at[s, lax.rem(at + k, GROUP)], frecv.at[k], y_send, y_recv, (to, peer(k)[1]))
        for k in ORDER:
            send(obuf.at[s, lax.rem(at + k, GROUP)], orecv.at[s, k - 1], o_send.at[s], o_recv.at[s], peer(k))
        wait_all(orecv.at[s], o_recv.at[s])
        for k in range(GROUP - 1):
            total = total + orecv[s, k].astype(F32)
        return total

    def own_cells():
        wait_all(frecv, y_recv)
        total = frecv[0].astype(F32)
        for k in range(1, GROUP):
            total = total + frecv[k].astype(F32)
        return widen(total)

    def row_cells():
        wait_all(frow, w_recv)
        wides = []
        for j in range(GROUP):
            total = frow[0, j].astype(F32)
            for k in range(1, GROUP):
                total = total + frow[k, j].astype(F32)
            prod[j] = total
            wides.append(widen(total))
        return jnp.concatenate(wides, axis=1)

    def columns(product, j):
        return product[:, part_of(j, block)]

    arrive_maps = ("below", "above", "spread")

    @pl.when(ly == 0)
    def _():
        scatter(0, r, row_peer, lambda j: const[j])
        for name in arrive_maps:
            arrive(name)
        turn_spread()
        order_spread(by_r)
        sums = add_up(0, 1, scattered(0, r), bbuf, brecv, col_peer)
        sall[r] = sums.astype(BF16)
        gather_into(sall, r, row_peer, send_sem.at[0, 2], recv_sem.at[0, 2])
        arrive("panel")
        wide = widen(jnp.concatenate([sall[k].astype(F32) for k in range(GROUP)], axis=1))
        mine = dot_nt(wide, qown[...])
        vown[z] = jnp.concatenate([mine, jnp.zeros((ROWS, 128 - panel), F32)], axis=1).astype(BF16)
        gather_into(vown, z, col_peer, v_send, v_recv)
        values = jnp.concatenate([vown[k].astype(F32)[:, :panel] for k in range(GROUP)], axis=1)
        plain_end(values, r, row_peer)
        share_inverse(z, col_peer)
        share_spread(r, row_peer)
        fold(((below, lb_t, xb),))
        take_inverse()
        take_spread()

    @pl.when(ly == 1)
    def _():
        share_inverse(r, row_peer)
        for name in arrive_maps:
            arrive(name)
        fold(((above, la_t, xa), (below, lb_t, xb)))
        turn_spread()
        order_spread(by_z)
        take_inverse()
        wait_all(fone, one_recv)
        wide = widen(fone[...].astype(F32))
        scatter(0, r, row_peer, lambda j: const[j] - dot_nn(wide, columns(xa, j)))
        lead[0] = lead[0] - dot_nn(wide, la_t[...])
        plain_end(values_of(0, scattered(0, r), col_peer, row_peer), z, col_peer)
        share_product(xb)
        share_spread(z, col_peer)
        take_product()
        wide = row_cells()
        partial = dot_nn(wide, xo[...])
        held[...] = held[...] - dot_nn(widen(prod[r]), lb_t[...])
        values = values_of(1, partial, col_peer, row_peer)
        take_spread()
        out[...] = spread_out(1, values, held[...], 1.0, z, col_peer, 0, False)

    @pl.when(ly == 2)
    def _():
        share_inverse(z, col_peer)
        for name in arrive_maps:
            arrive(name)
        turn_spread()
        order_spread(by_r)
        share_spread(r, row_peer)
        fold(((above, la_t, xa), (below, lb_t, xb)))
        take_inverse()
        take_spread()
        wait_all(fone, one_recv)
        wide = widen(fone[...].astype(F32))
        scatter(0, z, col_peer, lambda j: const[j] - dot_nn(wide, columns(xa, j)))
        lead[0] = lead[0] - dot_nn(wide, la_t[...])
        values = values_of(0, scattered(0, z), row_peer, col_peer)
        held[...] = spread_out(0, values, lead[0], -1.0, r, row_peer, 3, True)
        wait_all(frow, y_send)

    @pl.when(ly == 3)
    def _():
        share_inverse(r, row_peer)
        for k in ORDER:
            send(const.at[lax.rem(r + k, GROUP)], crow.at[k - 1], bulk_send.at[C_AT], bulk_recv.at[C_AT], row_peer(k))
        for name in arrive_maps:
            arrive(name)
        turn_spread()
        order_spread(by_z)
        share_spread(z, col_peer)
        fold(((above, la_t, xa),))
        share_product(xa)
        wait_all(bulk[C_AT], bulk_recv.at[C_AT])
        known = const[r]
        for k in range(GROUP - 1):
            known = known + crow[k]
        crow[0] = known
        take_inverse()
        take_product()
        wide = row_cells()
        partial = crow[0] - dot_nn(wide, xo[...])
        lead[0] = lead[0] - dot_nn(widen(prod[r]), la_t[...])
        values = values_of(0, partial, col_peer, row_peer)
        take_spread()
        out[...] = spread_out(0, values, lead[0], -1.0, z, col_peer, 2, False)

    @pl.when(even)
    def _():
        wide = own_cells()
        scatter(1, z, col_peer, lambda j: dot_nn(wide, columns(xb, j)))
        held[...] = held[...] - dot_nn(wide, lb_t[...])
        values = values_of(1, scattered(1, z), row_peer, col_peer)

        @pl.when(ly == 2)
        def _():
            out[...] = spread_out(1, values, held[...], 1.0, r, row_peer, 1, True)
            wait_all(frow, y_send)

        @pl.when(ly == 0)
        def _():
            out[...] = spread_out(1, values, held[...], 1.0, r, row_peer, None, False)

    wait_all(bulk[Q_AT], bulk_send.at[Q_AT])
    wait_all(bulk[P_AT], bulk_send.at[P_AT])

    def left(s, phases):
        for phase in phases:
            wait_all((arecv, brecv, crecv)[phase].at[s], send_sem.at[s, phase])

    @pl.when(ly == 0)
    def _():
        left(0, (0, 1, 2))
        wait_all(vown.at[pl.ds(0, GROUP - 1)], v_send)
        left(1, (0, 1, 2))
        wait_all(orecv.at[1], o_send.at[1])

    @pl.when(ly == 1)
    def _():
        left(0, (0, 1, 2))
        left(1, (1, 2))
        wait_all(bulk[X_AT], bulk_send.at[X_AT])
        wait_all(frecv, y_send)
        wait_all(orecv.at[1], o_send.at[1])

    @pl.when(ly < 2)
    def _():
        wait_all(vall.at[pl.ds(0, GROUP - 1)], send_sem.at[0, 3])
        wait_all(fone, one_send)

    @pl.when(ly == 2)
    def _():
        left(0, (0, 1, 2))
        left(1, (0, 1, 2))
        for s in range(2):
            wait_all(orecv.at[s], o_send.at[s])

    @pl.when(ly == 3)
    def _():
        left(0, (1, 2))
        wait_all(bulk[X_AT], bulk_send.at[X_AT])
        wait_all(bulk[C_AT], bulk_send.at[C_AT])
        wait_all(frecv, y_send)
        wait_all(orecv.at[0], o_send.at[0])


def local(right_sides, leaf, above, below, gather, inverse, spread, owner):
    depth = lax.axis_size("layer")
    _, _, count, cells = right_sides.shape
    panel, sep = inverse.shape[2], inverse.shape[3]
    block = sep // GROUP
    vmem = pl.BlockSpec(memory_space=pltpu.VMEM)
    hbm = pl.BlockSpec(memory_space=pl.ANY)
    dma = pltpu.SemaphoreType.DMA
    slot = jnp.arange(sep // panel, dtype=jnp.int32)
    slots = jnp.sum(jnp.where(owner[0][:, None] == slot[None, :], slot[:, None], 0), axis=0)
    V = pltpu.VMEM
    out = pl.pallas_call(
        functools.partial(kernel, depth, cells, sep, panel),
        out_shape=jax.ShapeDtypeStruct((ROWS, cells), F32),
        in_specs=[pl.BlockSpec(memory_space=pltpu.SMEM), vmem] + [hbm] * 6,
        out_specs=vmem,
        scratch_shapes=[
            V((cells, 2 * cells), BF16),
            V((cells, 2 * cells), BF16),
            V((cells, 2 * cells), BF16),
            V((sep, 2 * cells), BF16),
            V((block, 2 * block), BF16),
            V((2, cells, sep), BF16),
            V((2 * cells, cells), BF16),
            V((2 * cells, cells), BF16),
            V((2 * cells, cells), BF16),
            V((2 * cells, sep), BF16),
            V((2 * cells, sep), BF16),
            V((GROUP * 2 * cells, block), BF16),
            V((2 * block, block), BF16),
            V((2, sep // panel, panel, cells), BF16),
            V((2, sep, cells), BF16),
            V((2 * block, GROUP * cells), BF16),
            V((panel, 2 * sep), BF16),
            V((2, GROUP, ROWS, block), BF16),
            V((2, GROUP - 1, ROWS, block), BF16),
            V((2, ROWS, block), BF16),
            V((2, GROUP - 1, ROWS, block), BF16),
            V((2, ROWS, block), BF16),
            V((2, GROUP - 1, ROWS, block), BF16),
            V((GROUP - 1, ROWS, block), F32),
            V((GROUP, ROWS, block), BF16),
            V((GROUP, ROWS, 128), BF16),
            V((GROUP, ROWS, block), BF16),
            V((ROWS, cells), BF16),
            V((ROWS, cells), BF16),
            V((2, GROUP, ROWS, cells), BF16),
            V((2, GROUP - 1, ROWS, cells), BF16),
            V((GROUP, ROWS, cells), BF16),
            V((GROUP, GROUP, ROWS, cells), BF16),
            V((GROUP, ROWS, block), F32),
            V((1, ROWS, cells), F32),
            V((ROWS, cells), F32),
            V((GROUP, ROWS, cells), F32),
            dma((13,)),
            dma((2, 4)), dma((2, 4)),
            dma((4,)), dma((4,)),
            dma, dma,
            dma, dma, dma,
            dma((2,)), dma((2,)),
            dma, dma,
        ],
        compiler_params=pltpu.CompilerParams(
            collective_id=0, has_side_effects=True, vmem_limit_bytes=60 * 2**20),
        name="sweep",
    )(slots, right_sides.reshape(ROWS, cells), leaf[0], above[0], below[0], gather[0], inverse[0], spread[0])
    return out.reshape(1, 2, count, cells)


def solution(mesh):
    return jax.shard_map(
        local,
        mesh=mesh,
        in_specs=(
            P("layer", None, None, "front"),
            P("layer", None, "front", None),
            P("layer", None, "front", None),
            P("layer", None, "front", None),
            P("layer", None, None, "front"),
            P("layer", None, "front", None),
            P("layer", None, "front", None),
            P("layer", None),
        ),
        out_specs=P("layer", None, None, "front"),
        check_vma=False,
    )
```

```python
import functools

import jax
import jax.numpy as jnp
from jax import lax
from jax.experimental import pallas as pl
from jax.experimental.pallas import tpu as pltpu
from jax.sharding import PartitionSpec as P

MESH = pl.DeviceIdType.MESH
F32 = jnp.float32
BF16 = jnp.bfloat16
ROWS = 8
GROUP = 8
ORDER = (4, 3, 5, 2, 6, 1, 7)


def widen(v):
    turned = pltpu.roll(v, 4, 0)
    row = lax.broadcasted_iota(jnp.int32, v.shape, 0)
    turned = jnp.where(row < 4, -turned, turned)
    return jnp.concatenate([v, turned], axis=1).astype(BF16)


def dot_nt(a, b):
    return lax.dot_general(a, b, (((1,), (1,)), ((), ())), preferred_element_type=F32)


def dot_nn(a, b):
    return lax.dot_general(a, b, (((1,), (0,)), ((), ())), preferred_element_type=F32)


def expand(stack, n):
    top, low = stack[:n], stack[n:]
    return jnp.concatenate(
        [jnp.concatenate([top, -low], axis=1), jnp.concatenate([low, top], axis=1)], axis=0).astype(BF16)


def kernel(
    depth, cells, sep, panel,
    slots, rs, leaf_h, above_h, below_h, gather_h, inv_h, spread_h,
    out,
    leaf, above, below, gath, qmat, pnat, leaf_t, la_t, lb_t, xa, xb, xo, qt, pt, pts, po, qown,
    abuf, arecv, bbuf, brecv, cbuf, crecv, crow, sall, vown, vall, fbuf, fone, obuf, orecv, frecv, frow,
    const, lead, held, prod,
    load_sem, send_sem, recv_sem, bulk_send, bulk_recv, one_send, one_recv,
    y_send, y_recv, w_recv, o_send, o_recv, v_send, v_recv,
):
    ly = lax.axis_index("layer")
    me = lax.axis_index("front")
    z, r = me // GROUP, lax.rem(me, GROUP)
    block = sep // GROUP
    Q_AT, P_AT, X_AT, C_AT = range(4)

    def row_peer(k):
        return (ly, z * GROUP + lax.rem(r + k, GROUP))

    def col_peer(k):
        return (ly, lax.rem(z + k, GROUP) * GROUP + r)

    def wait_all(ref, sem):
        pltpu.make_async_copy(ref, ref, sem).wait()

    def send(src, dst, send_at, recv_at, to):
        pltpu.make_async_remote_copy(
            src_ref=src, dst_ref=dst, send_sem=send_at, recv_sem=recv_at, device_id=to, device_id_type=MESH).start()

    def part_of(index, size):
        return pl.ds(pl.multiple_of(index * size, 128 if size % 128 == 0 else 16), size)

    bulk = (
        qmat.at[pl.ds(0, (GROUP - 1) * panel), :],
        po.at[:, pl.ds(0, (GROUP - 1) * cells)],
        xo.at[pl.ds(0, (GROUP - 1) * 2 * cells), :],
        crow,
    )

    loads = {}
    n = 0
    for name, src, dst in (("leaf", leaf_h, leaf), ("gath", gather_h, gath), ("below", below_h, below), ("above", above_h, above)):
        loads[name] = []
        for part in range(2):
            copy = pltpu.make_async_copy(src.at[part], dst.at[:, pl.ds(part * cells, cells)], load_sem.at[n])
            copy.start()
            loads[name].append(copy)
            n += 1
    loads["spread"] = [pltpu.make_async_copy(spread_h, pnat, load_sem.at[n])]
    loads["spread"][0].start()
    n += 1
    even = lax.rem(ly, 2) == 0
    place = jnp.where(even, z, r)
    loads["own"], loads["panel"] = [], []
    for part in range(2):
        loads["own"].append(pltpu.make_async_copy(
            inv_h.at[part, :, part_of(place, block)],
            qmat.at[part_of(place, panel), pl.ds(part * block, block)], load_sem.at[n]))
        loads["panel"].append(pltpu.make_async_copy(inv_h.at[part], qown.at[:, pl.ds(part * sep, sep)], load_sem.at[n + 1]))
        n += 2
    for copy in loads["own"]:
        copy.start()

    @pl.when(ly == 0)
    def _():
        for copy in loads["panel"]:
            copy.start()

    def arrive(name):
        for copy in loads[name]:
            copy.wait()

    barrier = pltpu.get_barrier_semaphore()

    def greet(to):
        pl.semaphore_signal(barrier, inc=1, device_id=to, device_id_type=MESH)

    for k in range(1, GROUP):
        greet(row_peer(k))
        greet(col_peer(k))
    for low, along_row, along_col in ((0, False, True), (1, True, False), (2, True, True)):
        for mine, other in ((low, low + 1), (low + 1, low)):
            @pl.when(ly == mine)
            def _(other=other, along_row=along_row, along_col=along_col):
                greet((other, me))
                for k in range(1, GROUP):
                    if along_row:
                        greet((other, row_peer(k)[1]))
                    if along_col:
                        greet((other, col_peer(k)[1]))

    arrive("leaf")
    arrive("gath")
    first = dot_nt(widen(rs[...]), leaf[...])
    lead[0] = first
    wide = widen(first)
    for j in range(GROUP):
        const[j] = dot_nt(wide, gath[pl.ds(j * block, block), :])

    greeted = (GROUP, 2 * GROUP, 3 * GROUP - 1, 2 * GROUP - 1)
    extra = jnp.where(ly == 0, greeted[0], jnp.where(ly == 1, greeted[1], jnp.where(ly == 2, greeted[2], greeted[3])))
    pl.semaphore_wait(barrier, 2 * (GROUP - 1) + extra)

    def scatter(s, at, peer, term):
        for k in ORDER + (0,):
            j = lax.rem(at + k, GROUP)
            abuf[s, j] = term(j).astype(BF16)
            if k:
                send(abuf.at[s, j], arecv.at[s, k - 1], send_sem.at[s, 0], recv_sem.at[s, 0], peer(k))

    def scattered(s, at):
        wait_all(arecv.at[s], recv_sem.at[s, 0])
        total = abuf[s, at].astype(F32)
        for k in range(GROUP - 1):
            total = total + arecv[s, k].astype(F32)
        return total

    def add_up(s, phase, mine, buf, recv, peer):
        buf[s] = mine.astype(BF16)
        for k in ORDER:
            send(buf.at[s], recv.at[s, k - 1], send_sem.at[s, phase], recv_sem.at[s, phase], peer(k))
        wait_all(recv.at[s], recv_sem.at[s, phase])
        for k in range(GROUP - 1):
            mine = mine + recv[s, k].astype(F32)
        return mine

    def values_of(s, partial, sums_peer, values_peer, late=False):
        sums = add_up(s, 1, partial, bbuf, brecv, sums_peer)
        if late:
            take_inverse()
        return add_up(s, 2, dot_nn(widen(sums), qt[...]), cbuf, crecv, values_peer)

    def gather_into(ref, at, peer, send_at, recv_at, meanwhile=None):
        for k in ORDER:
            send(ref.at[at], ref.at[at], send_at, recv_at, peer(k))
        if meanwhile:
            meanwhile()
        wait_all(ref.at[pl.ds(0, GROUP - 1)], recv_at)

    def share_inverse(at, peer):
        for k in ORDER:
            for part in range(2):
                send(inv_h.at[part, :, part_of(lax.rem(at + k, GROUP), block)],
                     qmat.at[part_of(at, panel), pl.ds(part * block, block)],
                     bulk_send.at[Q_AT], bulk_recv.at[Q_AT], peer(k))

    def take_inverse():
        arrive("own")
        wait_all(bulk[Q_AT], bulk_recv.at[Q_AT])
        qt[...] = qmat[...].T

    def share_spread(at, peer):
        for k in ORDER:
            for part in range(2):
                send(pts.at[part, part_of(lax.rem(at + k, GROUP), block)],
                     po.at[pl.ds(part * block, block), part_of(at, cells)],
                     bulk_send.at[P_AT], bulk_recv.at[P_AT], peer(k))
        for part in range(2):
            po[pl.ds(part * block, block), part_of(at, cells)] = pts[part, part_of(at, block), :]

    def take_spread():
        wait_all(bulk[P_AT], bulk_recv.at[P_AT])

    def share_product(product, at, peer):
        for k in ORDER:
            send(product.at[:, part_of(lax.rem(at + k, GROUP), block)], xo.at[part_of(at, 2 * cells), :],
                 bulk_send.at[X_AT], bulk_recv.at[X_AT], peer(k))
        xo[part_of(at, 2 * cells), :] = product[:, part_of(at, block)]

    def take_product():
        wait_all(bulk[X_AT], bulk_recv.at[X_AT])

    def fold(pairs):
        leaf_t[...] = leaf[...].T
        leaf_stack = leaf_t[...]
        for coupling, folded, product in pairs:
            left = expand(coupling[...].T.astype(F32), cells)
            stack = dot_nn(left, leaf_stack)
            folded[...] = stack.astype(BF16)
            left = expand(stack, cells)
            for j in range(GROUP):
                product[:, j * block:(j + 1) * block] = dot_nt(left, gath[pl.ds(j * block, block), :]).astype(BF16)

    def turn_spread():
        for part in range(2):
            for j in range(GROUP):
                turned = pnat[part, :, j * block:(j + 1) * block].T
                per = block // panel
                pt[part, pl.ds(j * per, per)] = turned.reshape(per, panel, cells)

    def order_spread(order):
        for place, slot in enumerate(order):
            at = slots[slot]
            for part in range(2):
                pts[part, place * panel:(place + 1) * panel, :] = pt[part, at]

    by_z = range(GROUP * GROUP)
    by_r = [zz * GROUP + rr for rr in range(GROUP) for zz in range(GROUP)]

    def plain_end(values, at, peer):
        vall[at] = values.astype(BF16)
        gather_into(vall, at, peer, send_sem.at[0, 3], recv_sem.at[0, 3])
        wide = widen(jnp.concatenate([vall[k].astype(F32) for k in range(GROUP)], axis=1))
        forward = lead[0] - dot_nn(wide[:, :sep], pts[0]) - dot_nn(wide[:, sep:], pts[1])
        held[...] = forward
        fbuf[...] = forward.astype(BF16)
        send(fbuf, fone, one_send, one_recv, (ly + 1, me))

    def spread_out(s, values, own, sign, at, peer, to, whole):
        wide = widen(values)

        def pass_on(k):
            j = lax.rem(at + k, GROUP)
            if to is not None and not whole:
                send(obuf.at[s, j], frecv.at[k], y_send, y_recv, (to, peer(k)[1]))
            if k:
                send(obuf.at[s, j], orecv.at[s, k - 1], o_send.at[s], o_recv.at[s], peer(k))

        if whole:
            shares = sign * dot_nn(wide, po[...])
            for j in range(GROUP):
                prod[j] = shares[:, j * cells:(j + 1) * cells]
                obuf[s, j] = shares[:, j * cells:(j + 1) * cells].astype(BF16)
            total = own + prod[at]
            obuf[s, at] = total.astype(BF16)
            for k in ORDER + (0,):
                send(obuf.at[s], frow.at[k], y_send, w_recv, (to, peer(k)[1]))
            for k in ORDER:
                pass_on(k)
        else:
            for k in ORDER + (0,):
                j = lax.rem(at + k, GROUP)
                share = sign * dot_nn(wide, po[:, part_of(j, cells)])
                if not k:
                    share = total = own + share
                obuf[s, j] = share.astype(BF16)
                pass_on(k)
        wait_all(orecv.at[s], o_recv.at[s])
        for k in range(GROUP - 1):
            total = total + orecv[s, k].astype(F32)
        return total

    def own_cells():
        wait_all(frecv, y_recv)
        total = frecv[0].astype(F32)
        for k in range(1, GROUP):
            total = total + frecv[k].astype(F32)
        return widen(total)

    def group_cells():
        wait_all(frow, w_recv)
        wides = []
        for j in range(GROUP):
            total = frow[0, j].astype(F32)
            for k in range(1, GROUP):
                total = total + frow[k, j].astype(F32)
            prod[j] = total
            wides.append(widen(total))
        return jnp.concatenate(wides, axis=1)

    def columns(product, j):
        return product[:, part_of(j, block)]

    arrive_maps = ("below", "above", "spread")

    @pl.when(ly == 0)
    def _():
        scatter(0, r, row_peer, lambda j: const[j])
        for name in arrive_maps:
            arrive(name)
        turn_spread()
        order_spread(by_r)
        sums = add_up(0, 1, scattered(0, r), bbuf, brecv, col_peer)
        sall[r] = sums.astype(BF16)
        gather_into(sall, r, row_peer, send_sem.at[0, 2], recv_sem.at[0, 2])
        arrive("panel")
        wide = widen(jnp.concatenate([sall[k].astype(F32) for k in range(GROUP)], axis=1))
        mine = dot_nt(wide, qown[...])
        vown[z] = jnp.concatenate([mine, jnp.zeros((ROWS, 128 - panel), F32)], axis=1).astype(BF16)
        gather_into(vown, z, col_peer, v_send, v_recv, lambda: fold(((below, lb_t, xb),)))
        share_product(xb, z, col_peer)
        share_inverse(z, col_peer)
        values = jnp.concatenate([vown[k].astype(F32)[:, :panel] for k in range(GROUP)], axis=1)
        plain_end(values, r, row_peer)
        share_spread(r, row_peer)
        take_spread()
        take_product()
        wide = group_cells()
        partial = dot_nn(wide, xo[...])
        held[...] = held[...] - dot_nn(widen(prod[z]), lb_t[...])
        values = values_of(1, partial, row_peer, col_peer, True)
        out[...] = spread_out(1, values, held[...], 1.0, r, row_peer, None, False)

    @pl.when(ly == 1)
    def _():
        share_inverse(r, row_peer)
        for name in arrive_maps:
            arrive(name)
        fold(((above, la_t, xa), (below, lb_t, xb)))
        turn_spread()
        order_spread(by_z)
        take_inverse()
        wait_all(fone, one_recv)
        wide = widen(fone[...].astype(F32))
        scatter(0, r, row_peer, lambda j: const[j] - dot_nn(wide, columns(xa, j)))
        lead[0] = lead[0] - dot_nn(wide, la_t[...])
        plain_end(values_of(0, scattered(0, r), col_peer, row_peer), z, col_peer)
        share_product(xb, r, row_peer)
        share_spread(z, col_peer)
        take_product()
        wide = group_cells()
        partial = dot_nn(wide, xo[...])
        held[...] = held[...] - dot_nn(widen(prod[r]), lb_t[...])
        values = values_of(1, partial, col_peer, row_peer)
        take_spread()
        out[...] = spread_out(1, values, held[...], 1.0, z, col_peer, 0, True)

    @pl.when(ly == 2)
    def _():
        share_inverse(z, col_peer)
        for name in arrive_maps:
            arrive(name)
        turn_spread()
        order_spread(by_r)
        share_spread(r, row_peer)
        fold(((above, la_t, xa), (below, lb_t, xb)))
        take_inverse()
        take_spread()
        wait_all(fone, one_recv)
        wide = widen(fone[...].astype(F32))
        scatter(0, z, col_peer, lambda j: const[j] - dot_nn(wide, columns(xa, j)))
        lead[0] = lead[0] - dot_nn(wide, la_t[...])
        values = values_of(0, scattered(0, z), row_peer, col_peer)
        held[...] = spread_out(0, values, lead[0], -1.0, r, row_peer, 3, True)
        wait_all(frow, y_send)
        wide = own_cells()
        scatter(1, z, col_peer, lambda j: dot_nn(wide, columns(xb, j)))
        held[...] = held[...] - dot_nn(wide, lb_t[...])
        values = values_of(1, scattered(1, z), row_peer, col_peer)
        out[...] = spread_out(1, values, held[...], 1.0, r, row_peer, 1, True)
        wait_all(frow, y_send)

    @pl.when(ly == 3)
    def _():
        share_inverse(r, row_peer)
        for k in ORDER:
            send(const.at[lax.rem(r + k, GROUP)], crow.at[k - 1], bulk_send.at[C_AT], bulk_recv.at[C_AT], row_peer(k))
        for name in arrive_maps:
            arrive(name)
        turn_spread()
        order_spread(by_z)
        share_spread(z, col_peer)
        fold(((above, la_t, xa),))
        share_product(xa, r, row_peer)
        wait_all(bulk[C_AT], bulk_recv.at[C_AT])
        known = const[r]
        for k in range(GROUP - 1):
            known = known + crow[k]
        crow[0] = known
        take_inverse()
        take_product()
        wide = group_cells()
        partial = crow[0] - dot_nn(wide, xo[...])
        lead[0] = lead[0] - dot_nn(widen(prod[r]), la_t[...])
        values = values_of(0, partial, col_peer, row_peer)
        take_spread()
        out[...] = spread_out(0, values, lead[0], -1.0, z, col_peer, 2, False)

    wait_all(bulk[Q_AT], bulk_send.at[Q_AT])
    wait_all(bulk[P_AT], bulk_send.at[P_AT])

    def left(s, phases):
        for phase in phases:
            wait_all((arecv, brecv, crecv)[phase].at[s], send_sem.at[s, phase])

    @pl.when(ly == 0)
    def _():
        left(0, (0, 1, 2))
        wait_all(vown.at[pl.ds(0, GROUP - 1)], v_send)
        wait_all(bulk[X_AT], bulk_send.at[X_AT])
        left(1, (1, 2))
        wait_all(orecv.at[1], o_send.at[1])

    @pl.when(ly == 1)
    def _():
        left(0, (0, 1, 2))
        left(1, (1, 2))
        wait_all(bulk[X_AT], bulk_send.at[X_AT])
        wait_all(frow, y_send)
        wait_all(orecv.at[1], o_send.at[1])

    @pl.when(ly < 2)
    def _():
        wait_all(vall.at[pl.ds(0, GROUP - 1)], send_sem.at[0, 3])
        wait_all(fone, one_send)

    @pl.when(ly == 2)
    def _():
        left(0, (0, 1, 2))
        left(1, (0, 1, 2))
        for s in range(2):
            wait_all(orecv.at[s], o_send.at[s])

    @pl.when(ly == 3)
    def _():
        left(0, (1, 2))
        wait_all(bulk[X_AT], bulk_send.at[X_AT])
        wait_all(bulk[C_AT], bulk_send.at[C_AT])
        wait_all(frecv, y_send)
        wait_all(orecv.at[0], o_send.at[0])


def local(right_sides, leaf, above, below, gather, inverse, spread, owner):
    depth = lax.axis_size("layer")
    _, _, count, cells = right_sides.shape
    panel, sep = inverse.shape[2], inverse.shape[3]
    block = sep // GROUP
    vmem = pl.BlockSpec(memory_space=pltpu.VMEM)
    hbm = pl.BlockSpec(memory_space=pl.ANY)
    dma = pltpu.SemaphoreType.DMA
    slot = jnp.arange(sep // panel, dtype=jnp.int32)
    slots = jnp.sum(jnp.where(owner[0][:, None] == slot[None, :], slot[:, None], 0), axis=0)
    V = pltpu.VMEM
    out = pl.pallas_call(
        functools.partial(kernel, depth, cells, sep, panel),
        out_shape=jax.ShapeDtypeStruct((ROWS, cells), F32),
        in_specs=[pl.BlockSpec(memory_space=pltpu.SMEM), vmem] + [hbm] * 6,
        out_specs=vmem,
        scratch_shapes=[
            V((cells, 2 * cells), BF16),
            V((cells, 2 * cells), BF16),
            V((cells, 2 * cells), BF16),
            V((sep, 2 * cells), BF16),
            V((block, 2 * block), BF16),
            V((2, cells, sep), BF16),
            V((2 * cells, cells), BF16),
            V((2 * cells, cells), BF16),
            V((2 * cells, cells), BF16),
            V((2 * cells, sep), BF16),
            V((2 * cells, sep), BF16),
            V((GROUP * 2 * cells, block), BF16),
            V((2 * block, block), BF16),
            V((2, sep // panel, panel, cells), BF16),
            V((2, sep, cells), BF16),
            V((2 * block, GROUP * cells), BF16),
            V((panel, 2 * sep), BF16),
            V((2, GROUP, ROWS, block), BF16),
            V((2, GROUP - 1, ROWS, block), BF16),
            V((2, ROWS, block), BF16),
            V((2, GROUP - 1, ROWS, block), BF16),
            V((2, ROWS, block), BF16),
            V((2, GROUP - 1, ROWS, block), BF16),
            V((GROUP - 1, ROWS, block), F32),
            V((GROUP, ROWS, block), BF16),
            V((GROUP, ROWS, 128), BF16),
            V((GROUP, ROWS, block), BF16),
            V((ROWS, cells), BF16),
            V((ROWS, cells), BF16),
            V((2, GROUP, ROWS, cells), BF16),
            V((2, GROUP - 1, ROWS, cells), BF16),
            V((GROUP, ROWS, cells), BF16),
            V((GROUP, GROUP, ROWS, cells), BF16),
            V((GROUP, ROWS, block), F32),
            V((1, ROWS, cells), F32),
            V((ROWS, cells), F32),
            V((GROUP, ROWS, cells), F32),
            dma((13,)),
            dma((2, 4)), dma((2, 4)),
            dma((4,)), dma((4,)),
            dma, dma,
            dma, dma, dma,
            dma((2,)), dma((2,)),
            dma, dma,
        ],
        compiler_params=pltpu.CompilerParams(
            collective_id=0, has_side_effects=True, vmem_limit_bytes=60 * 2**20),
        name="sweep",
    )(slots, right_sides.reshape(ROWS, cells), leaf[0], above[0], below[0], gather[0], inverse[0], spread[0])
    return out.reshape(1, 2, count, cells)


def solution(mesh):
    return jax.shard_map(
        local,
        mesh=mesh,
        in_specs=(
            P("layer", None, None, "front"),
            P("layer", None, "front", None),
            P("layer", None, "front", None),
            P("layer", None, "front", None),
            P("layer", None, None, "front"),
            P("layer", None, "front", None),
            P("layer", None, "front", None),
            P("layer", None),
        ),
        out_specs=P("layer", None, None, "front"),
        check_vma=False,
    )
```

```python
import functools

import jax
import jax.numpy as jnp
from jax import lax
from jax.experimental import pallas as pl
from jax.experimental.pallas import tpu as pltpu
from jax.sharding import PartitionSpec as P

MESH = pl.DeviceIdType.MESH
F32 = jnp.float32
BF16 = jnp.bfloat16
ROWS = 8
GROUP = 8
ORDER = (4, 3, 5, 2, 6, 1, 7)


def widen(v):
    turned = pltpu.roll(v, 4, 0)
    row = lax.broadcasted_iota(jnp.int32, v.shape, 0)
    turned = jnp.where(row < 4, -turned, turned)
    return jnp.concatenate([v, turned], axis=1).astype(BF16)


def dot_nt(a, b):
    return lax.dot_general(a, b, (((1,), (1,)), ((), ())), preferred_element_type=F32)


def dot_nn(a, b):
    return lax.dot_general(a, b, (((1,), (0,)), ((), ())), preferred_element_type=F32)


def expand(stack, n):
    top, low = stack[:n], stack[n:]
    return jnp.concatenate(
        [jnp.concatenate([top, -low], axis=1), jnp.concatenate([low, top], axis=1)], axis=0).astype(BF16)


def kernel(
    depth, cells, sep, panel,
    owner, rs, leaf_h, above_h, below_h, gather_h, inv_h, spread_h,
    out,
    leaf, above, below, gath, qmat, pnat, leaf_t, la_t, lb_t, xa, xb, xo, qt, pt, pts, po, qown,
    abuf, arecv, bbuf, brecv, cbuf, crecv, crow, sall, vown, vall, fbuf, fone, obuf, orecv, frecv, frow,
    const, lead, held, prod, table, slots,
    load_sem, send_sem, recv_sem, bulk_send, bulk_recv, one_send, one_recv,
    y_send, y_recv, w_recv, o_send, o_recv, v_send, v_recv,
):
    ly = lax.axis_index("layer")
    me = lax.axis_index("front")
    z, r = me // GROUP, lax.rem(me, GROUP)
    block = sep // GROUP
    Q_AT, P_AT, X_AT, C_AT = range(4)

    def row_peer(k):
        return (ly, z * GROUP + lax.rem(r + k, GROUP))

    def col_peer(k):
        return (ly, lax.rem(z + k, GROUP) * GROUP + r)

    def wait_all(ref, sem):
        pltpu.make_async_copy(ref, ref, sem).wait()

    def send(src, dst, send_at, recv_at, to):
        pltpu.make_async_remote_copy(
            src_ref=src, dst_ref=dst, send_sem=send_at, recv_sem=recv_at, device_id=to, device_id_type=MESH).start()

    def part_of(index, size):
        return pl.ds(pl.multiple_of(index * size, 128 if size % 128 == 0 else 16), size)

    bulk = (
        qmat.at[pl.ds(0, (GROUP - 1) * panel), :],
        po.at[:, pl.ds(0, (GROUP - 1) * cells)],
        xo.at[pl.ds(0, (GROUP - 1) * 2 * cells), :],
        crow,
    )

    loads = {}
    n = 0
    for name, src, dst in (("leaf", leaf_h, leaf), ("gath", gather_h, gath), ("below", below_h, below), ("above", above_h, above)):
        loads[name] = []
        for part in range(2):
            copy = pltpu.make_async_copy(src.at[part], dst.at[:, pl.ds(part * cells, cells)], load_sem.at[n])
            copy.start()
            loads[name].append(copy)
            n += 1
    loads["spread"] = [pltpu.make_async_copy(spread_h, pnat, load_sem.at[n])]
    loads["spread"][0].start()
    n += 1
    even = lax.rem(ly, 2) == 0
    place = jnp.where(even, z, r)
    loads["own"], loads["panel"] = [], []
    for part in range(2):
        loads["own"].append(pltpu.make_async_copy(
            inv_h.at[part, :, part_of(place, block)],
            qmat.at[part_of(place, panel), pl.ds(part * block, block)], load_sem.at[n]))
        loads["panel"].append(pltpu.make_async_copy(inv_h.at[part], qown.at[:, pl.ds(part * sep, sep)], load_sem.at[n + 1]))
        n += 2
    for copy in loads["own"]:
        copy.start()

    @pl.when(ly == 0)
    def _():
        for copy in loads["panel"]:
            copy.start()

    def arrive(name):
        for copy in loads[name]:
            copy.wait()

    barrier = pltpu.get_barrier_semaphore()

    def greet(to):
        pl.semaphore_signal(barrier, inc=1, device_id=to, device_id_type=MESH)

    for k in range(1, GROUP):
        greet(row_peer(k))
        greet(col_peer(k))
    for low, along_row, along_col in ((0, False, True), (1, True, False), (2, True, True)):
        for mine, other in ((low, low + 1), (low + 1, low)):
            @pl.when(ly == mine)
            def _(other=other, along_row=along_row, along_col=along_col):
                greet((other, me))
                for k in range(1, GROUP):
                    if along_row:
                        greet((other, row_peer(k)[1]))
                    if along_col:
                        greet((other, col_peer(k)[1]))

    count = sep // panel
    table[...] = jnp.full((1, 128), count, jnp.int32)
    table[:, :count] = owner[...]
    stored_in = jnp.broadcast_to(table[...], (128, 128)).T
    panel_at = lax.broadcasted_iota(jnp.int32, (128, 128), 0)
    slot_at = lax.broadcasted_iota(jnp.int32, (128, 128), 1)
    hit = (stored_in == slot_at) & (panel_at < count)
    table[...] = jnp.max(jnp.where(hit, panel_at, 0), axis=0, keepdims=True)
    loads["slots"] = [pltpu.make_async_copy(table, slots, load_sem.at[n])]
    loads["slots"][0].start()

    arrive("leaf")
    arrive("gath")
    first = dot_nt(widen(rs[...]), leaf[...])
    lead[0] = first
    wide = widen(first)
    for j in range(GROUP):
        const[j] = dot_nt(wide, gath[pl.ds(j * block, block), :])

    greeted = (GROUP, 2 * GROUP, 3 * GROUP - 1, 2 * GROUP - 1)
    extra = jnp.where(ly == 0, greeted[0], jnp.where(ly == 1, greeted[1], jnp.where(ly == 2, greeted[2], greeted[3])))
    pl.semaphore_wait(barrier, 2 * (GROUP - 1) + extra)

    def scatter(s, at, peer, term):
        for k in ORDER + (0,):
            j = lax.rem(at + k, GROUP)
            abuf[s, j] = term(j).astype(BF16)
            if k:
                send(abuf.at[s, j], arecv.at[s, k - 1], send_sem.at[s, 0], recv_sem.at[s, 0], peer(k))

    def scattered(s, at):
        wait_all(arecv.at[s], recv_sem.at[s, 0])
        total = abuf[s, at].astype(F32)
        for k in range(GROUP - 1):
            total = total + arecv[s, k].astype(F32)
        return total

    def add_up(s, phase, mine, buf, recv, peer):
        buf[s] = mine.astype(BF16)
        for k in ORDER:
            send(buf.at[s], recv.at[s, k - 1], send_sem.at[s, phase], recv_sem.at[s, phase], peer(k))
        wait_all(recv.at[s], recv_sem.at[s, phase])
        for k in range(GROUP - 1):
            mine = mine + recv[s, k].astype(F32)
        return mine

    def values_of(s, partial, sums_peer, values_peer, late=False):
        sums = add_up(s, 1, partial, bbuf, brecv, sums_peer)
        if late:
            take_inverse()
        return add_up(s, 2, dot_nn(widen(sums), qt[...]), cbuf, crecv, values_peer)

    def gather_into(ref, at, peer, send_at, recv_at, meanwhile=None):
        for k in ORDER:
            send(ref.at[at], ref.at[at], send_at, recv_at, peer(k))
        if meanwhile:
            meanwhile()
        wait_all(ref.at[pl.ds(0, GROUP - 1)], recv_at)

    def share_inverse(at, peer):
        for k in ORDER:
            for part in range(2):
                send(inv_h.at[part, :, part_of(lax.rem(at + k, GROUP), block)],
                     qmat.at[part_of(at, panel), pl.ds(part * block, block)],
                     bulk_send.at[Q_AT], bulk_recv.at[Q_AT], peer(k))

    def take_inverse():
        arrive("own")
        wait_all(bulk[Q_AT], bulk_recv.at[Q_AT])
        qt[...] = qmat[...].T

    def share_spread(at, peer):
        for k in ORDER:
            for part in range(2):
                send(pts.at[part, part_of(lax.rem(at + k, GROUP), block)],
                     po.at[pl.ds(part * block, block), part_of(at, cells)],
                     bulk_send.at[P_AT], bulk_recv.at[P_AT], peer(k))
        for part in range(2):
            po[pl.ds(part * block, block), part_of(at, cells)] = pts[part, part_of(at, block), :]

    def take_spread():
        wait_all(bulk[P_AT], bulk_recv.at[P_AT])

    def share_product(product, at, peer):
        for k in ORDER:
            send(product.at[:, part_of(lax.rem(at + k, GROUP), block)], xo.at[part_of(at, 2 * cells), :],
                 bulk_send.at[X_AT], bulk_recv.at[X_AT], peer(k))
        xo[part_of(at, 2 * cells), :] = product[:, part_of(at, block)]

    def take_product():
        wait_all(bulk[X_AT], bulk_recv.at[X_AT])

    def fold(pairs):
        leaf_t[...] = leaf[...].T
        leaf_stack = leaf_t[...]
        for coupling, folded, product in pairs:
            left = expand(coupling[...].T.astype(F32), cells)
            stack = dot_nn(left, leaf_stack)
            folded[...] = stack.astype(BF16)
            left = expand(stack, cells)
            for j in range(GROUP):
                product[:, j * block:(j + 1) * block] = dot_nt(left, gath[pl.ds(j * block, block), :]).astype(BF16)

    def turn_spread():
        for part in range(2):
            for j in range(GROUP):
                turned = pnat[part, :, j * block:(j + 1) * block].T
                per = block // panel
                pt[part, pl.ds(j * per, per)] = turned.reshape(per, panel, cells)

    def order_spread(order):
        arrive("slots")
        for place, slot in enumerate(order):
            at = slots[0, slot]
            for part in range(2):
                pts[part, place * panel:(place + 1) * panel, :] = pt[part, at]

    by_z = range(GROUP * GROUP)
    by_r = [zz * GROUP + rr for rr in range(GROUP) for zz in range(GROUP)]

    def plain_end(values, at, peer):
        vall[at] = values.astype(BF16)
        gather_into(vall, at, peer, send_sem.at[0, 3], recv_sem.at[0, 3])
        wide = widen(jnp.concatenate([vall[k].astype(F32) for k in range(GROUP)], axis=1))
        forward = lead[0] - dot_nn(wide[:, :sep], pts[0]) - dot_nn(wide[:, sep:], pts[1])
        held[...] = forward
        fbuf[...] = forward.astype(BF16)
        send(fbuf, fone, one_send, one_recv, (ly + 1, me))

    def spread_out(s, values, own, sign, at, peer, to, whole):
        wide = widen(values)

        def pass_on(k):
            j = lax.rem(at + k, GROUP)
            if to is not None and not whole:
                send(obuf.at[s, j], frecv.at[k], y_send, y_recv, (to, peer(k)[1]))
            if k:
                send(obuf.at[s, j], orecv.at[s, k - 1], o_send.at[s], o_recv.at[s], peer(k))

        if whole:
            shares = sign * dot_nn(wide, po[...])
            for j in range(GROUP):
                prod[j] = shares[:, j * cells:(j + 1) * cells]
                obuf[s, j] = shares[:, j * cells:(j + 1) * cells].astype(BF16)
            total = own + prod[at]
            obuf[s, at] = total.astype(BF16)
            for k in ORDER + (0,):
                send(obuf.at[s], frow.at[k], y_send, w_recv, (to, peer(k)[1]))
            for k in ORDER:
                pass_on(k)
        else:
            for k in ORDER + (0,):
                j = lax.rem(at + k, GROUP)
                share = sign * dot_nn(wide, po[:, part_of(j, cells)])
                if not k:
                    share = total = own + share
                obuf[s, j] = share.astype(BF16)
                pass_on(k)
        wait_all(orecv.at[s], o_recv.at[s])
        for k in range(GROUP - 1):
            total = total + orecv[s, k].astype(F32)
        return total

    def own_cells():
        wait_all(frecv, y_recv)
        total = frecv[0].astype(F32)
        for k in range(1, GROUP):
            total = total + frecv[k].astype(F32)
        return widen(total)

    def group_cells():
        wait_all(frow, w_recv)
        wides = []
        for j in range(GROUP):
            total = frow[0, j].astype(F32)
            for k in range(1, GROUP):
                total = total + frow[k, j].astype(F32)
            prod[j] = total
            wides.append(widen(total))
        return jnp.concatenate(wides, axis=1)

    def columns(product, j):
        return product[:, part_of(j, block)]

    arrive_maps = ("below", "above", "spread")

    @pl.when(ly == 0)
    def _():
        scatter(0, r, row_peer, lambda j: const[j])
        for name in arrive_maps:
            arrive(name)
        turn_spread()
        order_spread(by_r)
        sums = add_up(0, 1, scattered(0, r), bbuf, brecv, col_peer)
        sall[r] = sums.astype(BF16)
        gather_into(sall, r, row_peer, send_sem.at[0, 2], recv_sem.at[0, 2])
        arrive("panel")
        wide = widen(jnp.concatenate([sall[k].astype(F32) for k in range(GROUP)], axis=1))
        mine = dot_nt(wide, qown[...])
        vown[z] = jnp.concatenate([mine, jnp.zeros((ROWS, 128 - panel), F32)], axis=1).astype(BF16)
        gather_into(vown, z, col_peer, v_send, v_recv, lambda: fold(((below, lb_t, xb),)))
        share_product(xb, z, col_peer)
        share_inverse(z, col_peer)
        values = jnp.concatenate([vown[k].astype(F32)[:, :panel] for k in range(GROUP)], axis=1)
        plain_end(values, r, row_peer)
        share_spread(r, row_peer)
        take_spread()
        take_product()
        wide = group_cells()
        partial = dot_nn(wide, xo[...])
        held[...] = held[...] - dot_nn(widen(prod[z]), lb_t[...])
        values = values_of(1, partial, row_peer, col_peer, True)
        out[...] = spread_out(1, values, held[...], 1.0, r, row_peer, None, False)

    @pl.when(ly == 1)
    def _():
        share_inverse(r, row_peer)
        for name in arrive_maps:
            arrive(name)
        fold(((above, la_t, xa), (below, lb_t, xb)))
        turn_spread()
        order_spread(by_z)
        take_inverse()
        wait_all(fone, one_recv)
        wide = widen(fone[...].astype(F32))
        scatter(0, r, row_peer, lambda j: const[j] - dot_nn(wide, columns(xa, j)))
        lead[0] = lead[0] - dot_nn(wide, la_t[...])
        plain_end(values_of(0, scattered(0, r), col_peer, row_peer), z, col_peer)
        share_product(xb, r, row_peer)
        share_spread(z, col_peer)
        take_product()
        wide = group_cells()
        partial = dot_nn(wide, xo[...])
        held[...] = held[...] - dot_nn(widen(prod[r]), lb_t[...])
        values = values_of(1, partial, col_peer, row_peer)
        take_spread()
        out[...] = spread_out(1, values, held[...], 1.0, z, col_peer, 0, True)

    @pl.when(ly == 2)
    def _():
        share_inverse(z, col_peer)
        for name in arrive_maps:
            arrive(name)
        turn_spread()
        order_spread(by_r)
        share_spread(r, row_peer)
        fold(((above, la_t, xa), (below, lb_t, xb)))
        take_inverse()
        take_spread()
        wait_all(fone, one_recv)
        wide = widen(fone[...].astype(F32))
        scatter(0, z, col_peer, lambda j: const[j] - dot_nn(wide, columns(xa, j)))
        lead[0] = lead[0] - dot_nn(wide, la_t[...])
        values = values_of(0, scattered(0, z), row_peer, col_peer)
        held[...] = spread_out(0, values, lead[0], -1.0, r, row_peer, 3, True)
        wait_all(frow, y_send)
        wide = own_cells()
        scatter(1, z, col_peer, lambda j: dot_nn(wide, columns(xb, j)))
        held[...] = held[...] - dot_nn(wide, lb_t[...])
        values = values_of(1, scattered(1, z), row_peer, col_peer)
        out[...] = spread_out(1, values, held[...], 1.0, r, row_peer, 1, True)
        wait_all(frow, y_send)

    @pl.when(ly == 3)
    def _():
        share_inverse(r, row_peer)
        for k in ORDER:
            send(const.at[lax.rem(r + k, GROUP)], crow.at[k - 1], bulk_send.at[C_AT], bulk_recv.at[C_AT], row_peer(k))
        for name in arrive_maps:
            arrive(name)
        turn_spread()
        order_spread(by_z)
        share_spread(z, col_peer)
        fold(((above, la_t, xa),))
        share_product(xa, r, row_peer)
        wait_all(bulk[C_AT], bulk_recv.at[C_AT])
        known = const[r]
        for k in range(GROUP - 1):
            known = known + crow[k]
        crow[0] = known
        take_inverse()
        take_product()
        wide = group_cells()
        partial = crow[0] - dot_nn(wide, xo[...])
        lead[0] = lead[0] - dot_nn(widen(prod[r]), la_t[...])
        values = values_of(0, partial, col_peer, row_peer)
        take_spread()
        out[...] = spread_out(0, values, lead[0], -1.0, z, col_peer, 2, False)

    wait_all(bulk[Q_AT], bulk_send.at[Q_AT])
    wait_all(bulk[P_AT], bulk_send.at[P_AT])

    def left(s, phases):
        for phase in phases:
            wait_all((arecv, brecv, crecv)[phase].at[s], send_sem.at[s, phase])

    @pl.when(ly == 0)
    def _():
        left(0, (0, 1, 2))
        wait_all(vown.at[pl.ds(0, GROUP - 1)], v_send)
        wait_all(bulk[X_AT], bulk_send.at[X_AT])
        left(1, (1, 2))
        wait_all(orecv.at[1], o_send.at[1])

    @pl.when(ly == 1)
    def _():
        left(0, (0, 1, 2))
        left(1, (1, 2))
        wait_all(bulk[X_AT], bulk_send.at[X_AT])
        wait_all(frow, y_send)
        wait_all(orecv.at[1], o_send.at[1])

    @pl.when(ly < 2)
    def _():
        wait_all(vall.at[pl.ds(0, GROUP - 1)], send_sem.at[0, 3])
        wait_all(fone, one_send)

    @pl.when(ly == 2)
    def _():
        left(0, (0, 1, 2))
        left(1, (0, 1, 2))
        for s in range(2):
            wait_all(orecv.at[s], o_send.at[s])

    @pl.when(ly == 3)
    def _():
        left(0, (1, 2))
        wait_all(bulk[X_AT], bulk_send.at[X_AT])
        wait_all(bulk[C_AT], bulk_send.at[C_AT])
        wait_all(frecv, y_send)
        wait_all(orecv.at[0], o_send.at[0])


def local(right_sides, leaf, above, below, gather, inverse, spread, owner):
    depth = lax.axis_size("layer")
    _, _, count, cells = right_sides.shape
    panel, sep = inverse.shape[2], inverse.shape[3]
    block = sep // GROUP
    vmem = pl.BlockSpec(memory_space=pltpu.VMEM)
    hbm = pl.BlockSpec(memory_space=pl.ANY)
    dma = pltpu.SemaphoreType.DMA
    V = pltpu.VMEM
    out = pl.pallas_call(
        functools.partial(kernel, depth, cells, sep, panel),
        out_shape=pltpu.VMEM((ROWS, cells), F32),
        in_specs=[vmem, vmem] + [hbm] * 6,
        out_specs=vmem,
        scratch_shapes=[
            V((cells, 2 * cells), BF16),
            V((cells, 2 * cells), BF16),
            V((cells, 2 * cells), BF16),
            V((sep, 2 * cells), BF16),
            V((block, 2 * block), BF16),
            V((2, cells, sep), BF16),
            V((2 * cells, cells), BF16),
            V((2 * cells, cells), BF16),
            V((2 * cells, cells), BF16),
            V((2 * cells, sep), BF16),
            V((2 * cells, sep), BF16),
            V((GROUP * 2 * cells, block), BF16),
            V((2 * block, block), BF16),
            V((2, sep // panel, panel, cells), BF16),
            V((2, sep, cells), BF16),
            V((2 * block, GROUP * cells), BF16),
            V((panel, 2 * sep), BF16),
            V((2, GROUP, ROWS, block), BF16),
            V((2, GROUP - 1, ROWS, block), BF16),
            V((2, ROWS, block), BF16),
            V((2, GROUP - 1, ROWS, block), BF16),
            V((2, ROWS, block), BF16),
            V((2, GROUP - 1, ROWS, block), BF16),
            V((GROUP - 1, ROWS, block), F32),
            V((GROUP, ROWS, block), BF16),
            V((GROUP, ROWS, 128), BF16),
            V((GROUP, ROWS, block), BF16),
            V((ROWS, cells), BF16),
            V((ROWS, cells), BF16),
            V((2, GROUP, ROWS, cells), BF16),
            V((2, GROUP - 1, ROWS, cells), BF16),
            V((GROUP, ROWS, cells), BF16),
            V((GROUP, GROUP, ROWS, cells), BF16),
            V((GROUP, ROWS, block), F32),
            V((1, ROWS, cells), F32),
            V((ROWS, cells), F32),
            V((GROUP, ROWS, cells), F32),
            V((1, 128), jnp.int32),
            pltpu.SMEM((1, 128), jnp.int32),
            dma((14,)),
            dma((2, 4)), dma((2, 4)),
            dma((4,)), dma((4,)),
            dma, dma,
            dma, dma, dma,
            dma((2,)), dma((2,)),
            dma, dma,
        ],
        compiler_params=pltpu.CompilerParams(
            collective_id=0, has_side_effects=True, vmem_limit_bytes=60 * 2**20),
        name="sweep",
    )(owner, right_sides.reshape(ROWS, cells), leaf[0], above[0], below[0], gather[0], inverse[0], spread[0])
    return out.reshape(1, 2, count, cells)


def solution(mesh):
    return jax.shard_map(
        local,
        mesh=mesh,
        in_specs=(
            P("layer", None, None, "front"),
            P("layer", None, "front", None),
            P("layer", None, "front", None),
            P("layer", None, "front", None),
            P("layer", None, None, "front"),
            P("layer", None, "front", None),
            P("layer", None, "front", None),
            P("layer", None),
        ),
        out_specs=P("layer", None, None, "front"),
        check_vma=False,
    )
```

```python
import functools

import jax
import jax.numpy as jnp
from jax import lax
from jax.experimental import pallas as pl
from jax.experimental.pallas import tpu as pltpu
from jax.sharding import PartitionSpec as P

MESH = pl.DeviceIdType.MESH
F32 = jnp.float32
BF16 = jnp.bfloat16
ROWS = 8
GROUP = 8
ORDER = (4, 3, 5, 2, 6, 1, 7)


def widen(v):
    turned = pltpu.roll(v, 4, 0)
    row = lax.broadcasted_iota(jnp.int32, v.shape, 0)
    turned = jnp.where(row < 4, -turned, turned)
    return jnp.concatenate([v, turned], axis=1).astype(BF16)


def dot_nt(a, b):
    return lax.dot_general(a, b, (((1,), (1,)), ((), ())), preferred_element_type=F32)


def dot_nn(a, b):
    return lax.dot_general(a, b, (((1,), (0,)), ((), ())), preferred_element_type=F32)


def expand(stack, n):
    top, low = stack[:n], stack[n:]
    return jnp.concatenate(
        [jnp.concatenate([top, -low], axis=1), jnp.concatenate([low, top], axis=1)], axis=0).astype(BF16)


def kernel(
    depth, cells, sep, panel,
    owner, rs, leaf_h, above_h, below_h, gather_h, inv_h, spread_h,
    out,
    leaf, above, below, gath, qmat, pnat, leaf_t, la_t, lb_t, xa, xb, xo, qt, pt, pts, po, qown,
    abuf, arecv, bbuf, brecv, cbuf, crecv, crow, sall, vown, vall, fbuf, fone, obuf, orecv, frecv, frow,
    const, lead, held, prod, table, slots,
    load_sem, send_sem, recv_sem, bulk_send, bulk_recv, one_send, one_recv,
    y_send, y_recv, w_recv, o_send, o_recv, v_send, v_recv,
):
    ly = lax.axis_index("layer")
    me = lax.axis_index("front")
    z, r = me // GROUP, lax.rem(me, GROUP)
    block = sep // GROUP
    Q_AT, P_AT, X_AT, C_AT = range(4)

    def row_peer(k):
        return (ly, z * GROUP + lax.rem(r + k, GROUP))

    def col_peer(k):
        return (ly, lax.rem(z + k, GROUP) * GROUP + r)

    def wait_all(ref, sem):
        pltpu.make_async_copy(ref, ref, sem).wait()

    def send(src, dst, send_at, recv_at, to):
        pltpu.make_async_remote_copy(
            src_ref=src, dst_ref=dst, send_sem=send_at, recv_sem=recv_at, device_id=to, device_id_type=MESH).start()

    def part_of(index, size):
        return pl.ds(pl.multiple_of(index * size, 128 if size % 128 == 0 else 16), size)

    bulk = (
        qmat.at[pl.ds(0, (GROUP - 1) * panel), :],
        po.at[:, pl.ds(0, (GROUP - 1) * cells)],
        xo.at[pl.ds(0, (GROUP - 1) * 2 * cells), :],
        crow,
    )

    loads = {}
    n = 0
    for name, src, dst in (("leaf", leaf_h, leaf), ("gath", gather_h, gath), ("below", below_h, below), ("above", above_h, above)):
        loads[name] = []
        for part in range(2):
            copy = pltpu.make_async_copy(src.at[part], dst.at[:, pl.ds(part * cells, cells)], load_sem.at[n])
            copy.start()
            loads[name].append(copy)
            n += 1
    loads["spread"] = [pltpu.make_async_copy(spread_h, pnat, load_sem.at[n])]
    loads["spread"][0].start()
    n += 1
    even = lax.rem(ly, 2) == 0
    place = jnp.where(even, z, r)
    loads["own"], loads["panel"] = [], []
    for part in range(2):
        loads["own"].append(pltpu.make_async_copy(
            inv_h.at[part, :, part_of(place, block)],
            qmat.at[part_of(place, panel), pl.ds(part * block, block)], load_sem.at[n]))
        loads["panel"].append(pltpu.make_async_copy(inv_h.at[part], qown.at[:, pl.ds(part * sep, sep)], load_sem.at[n + 1]))
        n += 2
    for copy in loads["own"]:
        copy.start()

    @pl.when(ly == 0)
    def _():
        for copy in loads["panel"]:
            copy.start()

    def arrive(name):
        for copy in loads[name]:
            copy.wait()

    barrier = pltpu.get_barrier_semaphore()

    def greet(to):
        pl.semaphore_signal(barrier, inc=1, device_id=to, device_id_type=MESH)

    for k in range(1, GROUP):
        greet(row_peer(k))
        greet(col_peer(k))
    for low, along_row, along_col in ((0, False, True), (1, True, False), (2, True, True)):
        for mine, other in ((low, low + 1), (low + 1, low)):
            @pl.when(ly == mine)
            def _(other=other, along_row=along_row, along_col=along_col):
                greet((other, me))
                for k in range(1, GROUP):
                    if along_row:
                        greet((other, row_peer(k)[1]))
                    if along_col:
                        greet((other, col_peer(k)[1]))

    count = sep // panel
    table[...] = jnp.full((1, 128), count, jnp.int32)
    table[:, :count] = owner[...]
    stored_in = jnp.broadcast_to(table[...], (128, 128)).T
    panel_at = lax.broadcasted_iota(jnp.int32, (128, 128), 0)
    slot_at = lax.broadcasted_iota(jnp.int32, (128, 128), 1)
    hit = (stored_in == slot_at) & (panel_at < count)
    table[...] = jnp.max(jnp.where(hit, panel_at, 0), axis=0, keepdims=True)
    loads["slots"] = [pltpu.make_async_copy(table, slots, load_sem.at[n])]
    loads["slots"][0].start()

    arrive("leaf")
    arrive("gath")
    first = dot_nt(widen(rs[...]), leaf[...])
    lead[0] = first
    wide = widen(first)
    for j in range(GROUP):
        const[j] = dot_nt(wide, gath[pl.ds(j * block, block), :])

    greeted = (GROUP, 2 * GROUP, 3 * GROUP - 1, 2 * GROUP - 1)
    extra = jnp.where(ly == 0, greeted[0], jnp.where(ly == 1, greeted[1], jnp.where(ly == 2, greeted[2], greeted[3])))
    pl.semaphore_wait(barrier, 2 * (GROUP - 1) + extra)

    def scatter(s, at, peer, term):
        for k in ORDER + (0,):
            j = lax.rem(at + k, GROUP)
            abuf[s, j] = term(j).astype(BF16)
            if k:
                send(abuf.at[s, j], arecv.at[s, k - 1], send_sem.at[s, 0], recv_sem.at[s, 0], peer(k))

    def scattered(s, at):
        wait_all(arecv.at[s], recv_sem.at[s, 0])
        total = abuf[s, at].astype(F32)
        for k in range(GROUP - 1):
            total = total + arecv[s, k].astype(F32)
        return total

    def add_up(s, phase, mine, buf, recv, peer):
        buf[s] = mine.astype(BF16)
        for k in ORDER:
            send(buf.at[s], recv.at[s, k - 1], send_sem.at[s, phase], recv_sem.at[s, phase], peer(k))
        wait_all(recv.at[s], recv_sem.at[s, phase])
        for k in range(GROUP - 1):
            mine = mine + recv[s, k].astype(F32)
        return mine

    def values_of(s, partial, sums_peer, values_peer, late=False):
        sums = add_up(s, 1, partial, bbuf, brecv, sums_peer)
        if late:
            take_inverse()
        return add_up(s, 2, dot_nn(widen(sums), qt[...]), cbuf, crecv, values_peer)

    def gather_into(ref, at, peer, send_at, recv_at, meanwhile=None):
        for k in ORDER:
            send(ref.at[at], ref.at[at], send_at, recv_at, peer(k))
        if meanwhile:
            meanwhile()
        wait_all(ref.at[pl.ds(0, GROUP - 1)], recv_at)

    def share_inverse(at, peer):
        for k in ORDER:
            for part in range(2):
                send(inv_h.at[part, :, part_of(lax.rem(at + k, GROUP), block)],
                     qmat.at[part_of(at, panel), pl.ds(part * block, block)],
                     bulk_send.at[Q_AT], bulk_recv.at[Q_AT], peer(k))

    def take_inverse():
        arrive("own")
        wait_all(bulk[Q_AT], bulk_recv.at[Q_AT])
        qt[...] = qmat[...].T

    def share_spread(at, peer):
        for k in ORDER:
            for part in range(2):
                send(pts.at[part, part_of(lax.rem(at + k, GROUP), block)],
                     po.at[pl.ds(part * block, block), part_of(at, cells)],
                     bulk_send.at[P_AT], bulk_recv.at[P_AT], peer(k))
        for part in range(2):
            po[pl.ds(part * block, block), part_of(at, cells)] = pts[part, part_of(at, block), :]

    def take_spread():
        wait_all(bulk[P_AT], bulk_recv.at[P_AT])

    def share_product(product, at, peer):
        for k in ORDER:
            send(product.at[:, part_of(lax.rem(at + k, GROUP), block)], xo.at[part_of(at, 2 * cells), :],
                 bulk_send.at[X_AT], bulk_recv.at[X_AT], peer(k))
        xo[part_of(at, 2 * cells), :] = product[:, part_of(at, block)]

    def take_product():
        wait_all(bulk[X_AT], bulk_recv.at[X_AT])

    def fold(pairs):
        leaf_t[...] = leaf[...].T
        leaf_stack = leaf_t[...]
        for coupling, folded, product in pairs:
            left = expand(coupling[...].T.astype(F32), cells)
            stack = dot_nn(left, leaf_stack)
            folded[...] = stack.astype(BF16)
            left = expand(stack, cells)
            for j in range(GROUP):
                product[:, j * block:(j + 1) * block] = dot_nt(left, gath[pl.ds(j * block, block), :]).astype(BF16)

    def turn_spread():
        for part in range(2):
            for j in range(GROUP):
                turned = pnat[part, :, j * block:(j + 1) * block].T
                per = block // panel
                pt[part, pl.ds(j * per, per)] = turned.reshape(per, panel, cells)

    def order_spread(order):
        arrive("slots")
        for place, slot in enumerate(order):
            at = slots[0, slot]
            for part in range(2):
                pts[part, place * panel:(place + 1) * panel, :] = pt[part, at]

    by_z = range(GROUP * GROUP)
    by_r = [zz * GROUP + rr for rr in range(GROUP) for zz in range(GROUP)]

    def plain_end(values, at, peer):
        vall[at] = values.astype(BF16)
        gather_into(vall, at, peer, send_sem.at[0, 3], recv_sem.at[0, 3])
        wide = widen(jnp.concatenate([vall[k].astype(F32) for k in range(GROUP)], axis=1))
        forward = lead[0] - dot_nn(wide[:, :sep], pts[0]) - dot_nn(wide[:, sep:], pts[1])
        held[...] = forward
        fbuf[...] = forward.astype(BF16)
        send(fbuf, fone, one_send, one_recv, (ly + 1, me))

    def spread_out(s, values, own, sign, at, peer, to, whole):
        wide = widen(values)

        def pass_on(k):
            j = lax.rem(at + k, GROUP)
            if to is not None and not whole:
                send(obuf.at[s, j], frecv.at[k], y_send, y_recv, (to, peer(k)[1]))
            if k:
                send(obuf.at[s, j], orecv.at[s, k - 1], o_send.at[s], o_recv.at[s], peer(k))

        if whole:
            half = GROUP // 2
            for low in (0, half):
                shares = sign * dot_nn(wide, po[:, low * cells:(low + half) * cells])
                for i in range(half):
                    share = shares[:, i * cells:(i + 1) * cells]
                    prod[low + i] = share
                    obuf[s, low + i] = jnp.where(at == low + i, share + own, share).astype(BF16)
                for k in ORDER + (0,):
                    send(obuf.at[s, pl.ds(low, half)], frow.at[k, pl.ds(low, half)], y_send, w_recv, (to, peer(k)[1]))
            total = own + prod[at]
            for k in ORDER:
                pass_on(k)
        else:
            for k in ORDER + (0,):
                j = lax.rem(at + k, GROUP)
                share = sign * dot_nn(wide, po[:, part_of(j, cells)])
                if not k:
                    share = total = own + share
                obuf[s, j] = share.astype(BF16)
                pass_on(k)
        wait_all(orecv.at[s], o_recv.at[s])
        for k in range(GROUP - 1):
            total = total + orecv[s, k].astype(F32)
        return total

    def own_cells():
        wait_all(frecv, y_recv)
        total = frecv[0].astype(F32)
        for k in range(1, GROUP):
            total = total + frecv[k].astype(F32)
        return widen(total)

    def group_cells():
        wait_all(frow, w_recv)
        wides = []
        for j in range(GROUP):
            total = frow[0, j].astype(F32)
            for k in range(1, GROUP):
                total = total + frow[k, j].astype(F32)
            prod[j] = total
            wides.append(widen(total))
        return jnp.concatenate(wides, axis=1)

    def columns(product, j):
        return product[:, part_of(j, block)]

    arrive_maps = ("below", "above", "spread")

    @pl.when(ly == 0)
    def _():
        scatter(0, r, row_peer, lambda j: const[j])
        for name in arrive_maps:
            arrive(name)
        turn_spread()
        order_spread(by_r)
        sums = add_up(0, 1, scattered(0, r), bbuf, brecv, col_peer)
        sall[r] = sums.astype(BF16)
        gather_into(sall, r, row_peer, send_sem.at[0, 2], recv_sem.at[0, 2])
        arrive("panel")
        wide = widen(jnp.concatenate([sall[k].astype(F32) for k in range(GROUP)], axis=1))
        mine = dot_nt(wide, qown[...])
        vown[z] = jnp.concatenate([mine, jnp.zeros((ROWS, 128 - panel), F32)], axis=1).astype(BF16)
        gather_into(vown, z, col_peer, v_send, v_recv, lambda: fold(((below, lb_t, xb),)))
        share_product(xb, z, col_peer)
        share_inverse(z, col_peer)
        values = jnp.concatenate([vown[k].astype(F32)[:, :panel] for k in range(GROUP)], axis=1)
        plain_end(values, r, row_peer)
        share_spread(r, row_peer)
        take_spread()
        take_product()
        wide = group_cells()
        partial = dot_nn(wide, xo[...])
        held[...] = held[...] - dot_nn(widen(prod[z]), lb_t[...])
        values = values_of(1, partial, row_peer, col_peer, True)
        out[...] = spread_out(1, values, held[...], 1.0, r, row_peer, None, False)

    @pl.when(ly == 1)
    def _():
        share_inverse(r, row_peer)
        for name in arrive_maps:
            arrive(name)
        fold(((above, la_t, xa), (below, lb_t, xb)))
        turn_spread()
        order_spread(by_z)
        take_inverse()
        wait_all(fone, one_recv)
        wide = widen(fone[...].astype(F32))
        scatter(0, r, row_peer, lambda j: const[j] - dot_nn(wide, columns(xa, j)))
        lead[0] = lead[0] - dot_nn(wide, la_t[...])
        plain_end(values_of(0, scattered(0, r), col_peer, row_peer), z, col_peer)
        share_product(xb, r, row_peer)
        share_spread(z, col_peer)
        take_product()
        wide = group_cells()
        partial = dot_nn(wide, xo[...])
        held[...] = held[...] - dot_nn(widen(prod[r]), lb_t[...])
        values = values_of(1, partial, col_peer, row_peer)
        take_spread()
        out[...] = spread_out(1, values, held[...], 1.0, z, col_peer, 0, True)

    @pl.when(ly == 2)
    def _():
        share_inverse(z, col_peer)
        for name in arrive_maps:
            arrive(name)
        turn_spread()
        order_spread(by_r)
        share_spread(r, row_peer)
        fold(((above, la_t, xa), (below, lb_t, xb)))
        take_inverse()
        take_spread()
        wait_all(fone, one_recv)
        wide = widen(fone[...].astype(F32))
        scatter(0, z, col_peer, lambda j: const[j] - dot_nn(wide, columns(xa, j)))
        lead[0] = lead[0] - dot_nn(wide, la_t[...])
        values = values_of(0, scattered(0, z), row_peer, col_peer)
        held[...] = spread_out(0, values, lead[0], -1.0, r, row_peer, 3, True)
        wait_all(frow, y_send)
        wide = own_cells()
        scatter(1, z, col_peer, lambda j: dot_nn(wide, columns(xb, j)))
        held[...] = held[...] - dot_nn(wide, lb_t[...])
        values = values_of(1, scattered(1, z), row_peer, col_peer)
        out[...] = spread_out(1, values, held[...], 1.0, r, row_peer, 1, True)
        wait_all(frow, y_send)

    @pl.when(ly == 3)
    def _():
        share_inverse(r, row_peer)
        for k in ORDER:
            send(const.at[lax.rem(r + k, GROUP)], crow.at[k - 1], bulk_send.at[C_AT], bulk_recv.at[C_AT], row_peer(k))
        for name in arrive_maps:
            arrive(name)
        turn_spread()
        order_spread(by_z)
        share_spread(z, col_peer)
        fold(((above, la_t, xa),))
        share_product(xa, r, row_peer)
        wait_all(bulk[C_AT], bulk_recv.at[C_AT])
        known = const[r]
        for k in range(GROUP - 1):
            known = known + crow[k]
        crow[0] = known
        take_inverse()
        take_product()
        wide = group_cells()
        partial = crow[0] - dot_nn(wide, xo[...])
        lead[0] = lead[0] - dot_nn(widen(prod[r]), la_t[...])
        values = values_of(0, partial, col_peer, row_peer)
        take_spread()
        out[...] = spread_out(0, values, lead[0], -1.0, z, col_peer, 2, False)

    wait_all(bulk[Q_AT], bulk_send.at[Q_AT])
    wait_all(bulk[P_AT], bulk_send.at[P_AT])

    def left(s, phases):
        for phase in phases:
            wait_all((arecv, brecv, crecv)[phase].at[s], send_sem.at[s, phase])

    @pl.when(ly == 0)
    def _():
        left(0, (0, 1, 2))
        wait_all(vown.at[pl.ds(0, GROUP - 1)], v_send)
        wait_all(bulk[X_AT], bulk_send.at[X_AT])
        left(1, (1, 2))
        wait_all(orecv.at[1], o_send.at[1])

    @pl.when(ly == 1)
    def _():
        left(0, (0, 1, 2))
        left(1, (1, 2))
        wait_all(bulk[X_AT], bulk_send.at[X_AT])
        wait_all(frow, y_send)
        wait_all(orecv.at[1], o_send.at[1])

    @pl.when(ly < 2)
    def _():
        wait_all(vall.at[pl.ds(0, GROUP - 1)], send_sem.at[0, 3])
        wait_all(fone, one_send)

    @pl.when(ly == 2)
    def _():
        left(0, (0, 1, 2))
        left(1, (0, 1, 2))
        for s in range(2):
            wait_all(orecv.at[s], o_send.at[s])

    @pl.when(ly == 3)
    def _():
        left(0, (1, 2))
        wait_all(bulk[X_AT], bulk_send.at[X_AT])
        wait_all(bulk[C_AT], bulk_send.at[C_AT])
        wait_all(frecv, y_send)
        wait_all(orecv.at[0], o_send.at[0])


def local(right_sides, leaf, above, below, gather, inverse, spread, owner):
    depth = lax.axis_size("layer")
    _, _, count, cells = right_sides.shape
    panel, sep = inverse.shape[2], inverse.shape[3]
    block = sep // GROUP
    vmem = pl.BlockSpec(memory_space=pltpu.VMEM)
    hbm = pl.BlockSpec(memory_space=pl.ANY)
    dma = pltpu.SemaphoreType.DMA
    V = pltpu.VMEM
    out = pl.pallas_call(
        functools.partial(kernel, depth, cells, sep, panel),
        out_shape=pltpu.VMEM((ROWS, cells), F32),
        in_specs=[vmem, vmem] + [hbm] * 6,
        out_specs=vmem,
        scratch_shapes=[
            V((cells, 2 * cells), BF16),
            V((cells, 2 * cells), BF16),
            V((cells, 2 * cells), BF16),
            V((sep, 2 * cells), BF16),
            V((block, 2 * block), BF16),
            V((2, cells, sep), BF16),
            V((2 * cells, cells), BF16),
            V((2 * cells, cells), BF16),
            V((2 * cells, cells), BF16),
            V((2 * cells, sep), BF16),
            V((2 * cells, sep), BF16),
            V((GROUP * 2 * cells, block), BF16),
            V((2 * block, block), BF16),
            V((2, sep // panel, panel, cells), BF16),
            V((2, sep, cells), BF16),
            V((2 * block, GROUP * cells), BF16),
            V((panel, 2 * sep), BF16),
            V((2, GROUP, ROWS, block), BF16),
            V((2, GROUP - 1, ROWS, block), BF16),
            V((2, ROWS, block), BF16),
            V((2, GROUP - 1, ROWS, block), BF16),
            V((2, ROWS, block), BF16),
            V((2, GROUP - 1, ROWS, block), BF16),
            V((GROUP - 1, ROWS, block), F32),
            V((GROUP, ROWS, block), BF16),
            V((GROUP, ROWS, 128), BF16),
            V((GROUP, ROWS, block), BF16),
            V((ROWS, cells), BF16),
            V((ROWS, cells), BF16),
            V((2, GROUP, ROWS, cells), BF16),
            V((2, GROUP - 1, ROWS, cells), BF16),
            V((GROUP, ROWS, cells), BF16),
            V((GROUP, GROUP, ROWS, cells), BF16),
            V((GROUP, ROWS, block), F32),
            V((1, ROWS, cells), F32),
            V((ROWS, cells), F32),
            V((GROUP, ROWS, cells), F32),
            V((1, 128), jnp.int32),
            pltpu.SMEM((1, 128), jnp.int32),
            dma((14,)),
            dma((2, 4)), dma((2, 4)),
            dma((4,)), dma((4,)),
            dma, dma,
            dma, dma, dma,
            dma((2,)), dma((2,)),
            dma, dma,
        ],
        compiler_params=pltpu.CompilerParams(
            collective_id=0, has_side_effects=True, vmem_limit_bytes=60 * 2**20),
        name="sweep",
    )(owner, right_sides.reshape(ROWS, cells), leaf[0], above[0], below[0], gather[0], inverse[0], spread[0])
    return out.reshape(1, 2, count, cells)


def solution(mesh):
    return jax.shard_map(
        local,
        mesh=mesh,
        in_specs=(
            P("layer", None, None, "front"),
            P("layer", None, "front", None),
            P("layer", None, "front", None),
            P("layer", None, "front", None),
            P("layer", None, None, "front"),
            P("layer", None, "front", None),
            P("layer", None, "front", None),
            P("layer", None),
        ),
        out_specs=P("layer", None, None, "front"),
        check_vma=False,
    )
```

```python
import functools

import jax
import jax.numpy as jnp
from jax import lax
from jax.experimental import pallas as pl
from jax.experimental.pallas import tpu as pltpu
from jax.sharding import PartitionSpec as P

MESH = pl.DeviceIdType.MESH
F32 = jnp.float32
BF16 = jnp.bfloat16
ROWS = 8
GROUP = 8
ORDER = (4, 3, 5, 2, 6, 1, 7)


def widen(v):
    turned = pltpu.roll(v, 4, 0)
    row = lax.broadcasted_iota(jnp.int32, v.shape, 0)
    turned = jnp.where(row < 4, -turned, turned)
    return jnp.concatenate([v, turned], axis=1).astype(BF16)


def dot_nt(a, b):
    return lax.dot_general(a, b, (((1,), (1,)), ((), ())), preferred_element_type=F32)


def dot_nn(a, b):
    return lax.dot_general(a, b, (((1,), (0,)), ((), ())), preferred_element_type=F32)


def expand(stack, n):
    top, low = stack[:n], stack[n:]
    return jnp.concatenate(
        [jnp.concatenate([top, -low], axis=1), jnp.concatenate([low, top], axis=1)], axis=0).astype(BF16)


def kernel(
    depth, cells, sep, panel,
    owner, rs, leaf_h, above_h, below_h, gather_h, inv_h, spread_h,
    out,
    leaf, above, below, gath, qmat, pnat, leaf_t, la_t, lb_t, xa, xb, xo, qt, pt, pts, po, qown, qown_t,
    abuf, arecv, bbuf, brecv, cbuf, crecv, crow, sall, vown, vall, fbuf, fone, obuf, orecv, frecv, frow,
    const, lead, held, prod, table, slots,
    load_sem, send_sem, recv_sem, bulk_send, bulk_recv, one_send, one_recv,
    y_send, y_recv, w_recv, o_send, o_recv, v_send, v_recv,
):
    ly = lax.axis_index("layer")
    me = lax.axis_index("front")
    z, r = me // GROUP, lax.rem(me, GROUP)
    block = sep // GROUP
    Q_AT, P_AT, X_AT, C_AT = range(4)

    def row_peer(k):
        return (ly, z * GROUP + lax.rem(r + k, GROUP))

    def col_peer(k):
        return (ly, lax.rem(z + k, GROUP) * GROUP + r)

    def wait_all(ref, sem):
        pltpu.make_async_copy(ref, ref, sem).wait()

    def send(src, dst, send_at, recv_at, to):
        pltpu.make_async_remote_copy(
            src_ref=src, dst_ref=dst, send_sem=send_at, recv_sem=recv_at, device_id=to, device_id_type=MESH).start()

    def part_of(index, size):
        return pl.ds(pl.multiple_of(index * size, 128 if size % 128 == 0 else 16), size)

    bulk = (
        qmat.at[pl.ds(0, (GROUP - 1) * panel), :],
        po.at[:, pl.ds(0, (GROUP - 1) * cells)],
        xo.at[pl.ds(0, (GROUP - 1) * 2 * cells), :],
        crow,
    )

    loads = {}
    n = 0
    for name, src, dst in (("leaf", leaf_h, leaf), ("gath", gather_h, gath), ("below", below_h, below), ("above", above_h, above)):
        loads[name] = []
        for part in range(2):
            copy = pltpu.make_async_copy(src.at[part], dst.at[:, pl.ds(part * cells, cells)], load_sem.at[n])
            copy.start()
            loads[name].append(copy)
            n += 1
    loads["spread"] = [pltpu.make_async_copy(spread_h, pnat, load_sem.at[n])]
    loads["spread"][0].start()
    n += 1
    even = lax.rem(ly, 2) == 0
    place = jnp.where(even, z, r)
    loads["own"], loads["panel"] = [], []
    for part in range(2):
        loads["own"].append(pltpu.make_async_copy(
            inv_h.at[part, :, part_of(place, block)],
            qmat.at[part_of(place, panel), pl.ds(part * block, block)], load_sem.at[n]))
        loads["panel"].append(pltpu.make_async_copy(inv_h.at[part], qown.at[:, pl.ds(part * sep, sep)], load_sem.at[n + 1]))
        n += 2
    for copy in loads["own"]:
        copy.start()

    @pl.when(ly == 0)
    def _():
        for copy in loads["panel"]:
            copy.start()

    def arrive(name):
        for copy in loads[name]:
            copy.wait()

    barrier = pltpu.get_barrier_semaphore()

    def greet(to):
        pl.semaphore_signal(barrier, inc=1, device_id=to, device_id_type=MESH)

    for k in range(1, GROUP):
        greet(row_peer(k))
        greet(col_peer(k))
    for low, along_row, along_col in ((0, False, True), (1, True, False), (2, True, True)):
        for mine, other in ((low, low + 1), (low + 1, low)):
            @pl.when(ly == mine)
            def _(other=other, along_row=along_row, along_col=along_col):
                greet((other, me))
                for k in range(1, GROUP):
                    if along_row:
                        greet((other, row_peer(k)[1]))
                    if along_col:
                        greet((other, col_peer(k)[1]))

    count = sep // panel
    table[...] = jnp.full((1, 128), count, jnp.int32)
    table[:, :count] = owner[...]
    stored_in = jnp.broadcast_to(table[...], (128, 128)).T
    panel_at = lax.broadcasted_iota(jnp.int32, (128, 128), 0)
    slot_at = lax.broadcasted_iota(jnp.int32, (128, 128), 1)
    hit = (stored_in == slot_at) & (panel_at < count)
    table[...] = jnp.max(jnp.where(hit, panel_at, 0), axis=0, keepdims=True)
    loads["slots"] = [pltpu.make_async_copy(table, slots, load_sem.at[n])]
    loads["slots"][0].start()

    arrive("leaf")
    arrive("gath")
    first = dot_nt(widen(rs[...]), leaf[...])
    lead[0] = first
    wide = widen(first)
    for j in range(GROUP):
        const[j] = dot_nt(wide, gath[pl.ds(j * block, block), :])

    greeted = (GROUP, 2 * GROUP, 3 * GROUP - 1, 2 * GROUP - 1)
    extra = jnp.where(ly == 0, greeted[0], jnp.where(ly == 1, greeted[1], jnp.where(ly == 2, greeted[2], greeted[3])))
    pl.semaphore_wait(barrier, 2 * (GROUP - 1) + extra)

    def scatter(s, at, peer, term):
        for k in ORDER + (0,):
            j = lax.rem(at + k, GROUP)
            abuf[s, j] = term(j).astype(BF16)
            if k:
                send(abuf.at[s, j], arecv.at[s, k - 1], send_sem.at[s, 0], recv_sem.at[s, 0], peer(k))

    def scattered(s, at):
        wait_all(arecv.at[s], recv_sem.at[s, 0])
        total = abuf[s, at].astype(F32)
        for k in range(GROUP - 1):
            total = total + arecv[s, k].astype(F32)
        return total

    def add_up(s, phase, mine, buf, recv, peer):
        buf[s] = mine.astype(BF16)
        for k in ORDER:
            send(buf.at[s], recv.at[s, k - 1], send_sem.at[s, phase], recv_sem.at[s, phase], peer(k))
        wait_all(recv.at[s], recv_sem.at[s, phase])
        for k in range(GROUP - 1):
            mine = mine + recv[s, k].astype(F32)
        return mine

    def values_of(s, partial, sums_peer, values_peer, late=False):
        sums = add_up(s, 1, partial, bbuf, brecv, sums_peer)
        if late:
            take_inverse()
        return add_up(s, 2, dot_nn(widen(sums), qt[...]), cbuf, crecv, values_peer)

    def gather_into(ref, at, peer, send_at, recv_at, meanwhile=None):
        for k in ORDER:
            send(ref.at[at], ref.at[at], send_at, recv_at, peer(k))
        if meanwhile:
            meanwhile()
        wait_all(ref.at[pl.ds(0, GROUP - 1)], recv_at)

    def share_inverse(at, peer):
        for k in ORDER:
            for part in range(2):
                send(inv_h.at[part, :, part_of(lax.rem(at + k, GROUP), block)],
                     qmat.at[part_of(at, panel), pl.ds(part * block, block)],
                     bulk_send.at[Q_AT], bulk_recv.at[Q_AT], peer(k))

    def take_inverse():
        arrive("own")
        wait_all(bulk[Q_AT], bulk_recv.at[Q_AT])
        qt[...] = qmat[...].T

    def share_spread(at, peer):
        for k in ORDER:
            for part in range(2):
                send(pts.at[part, part_of(lax.rem(at + k, GROUP), block)],
                     po.at[pl.ds(part * block, block), part_of(at, cells)],
                     bulk_send.at[P_AT], bulk_recv.at[P_AT], peer(k))
        for part in range(2):
            po[pl.ds(part * block, block), part_of(at, cells)] = pts[part, part_of(at, block), :]

    def take_spread():
        wait_all(bulk[P_AT], bulk_recv.at[P_AT])

    def share_product(product, at, peer):
        for k in ORDER:
            send(product.at[:, part_of(lax.rem(at + k, GROUP), block)], xo.at[part_of(at, 2 * cells), :],
                 bulk_send.at[X_AT], bulk_recv.at[X_AT], peer(k))
        xo[part_of(at, 2 * cells), :] = product[:, part_of(at, block)]

    def take_product():
        wait_all(bulk[X_AT], bulk_recv.at[X_AT])

    def fold(pairs):
        leaf_t[...] = leaf[...].T
        leaf_stack = leaf_t[...]
        for coupling, folded, product in pairs:
            left = expand(coupling[...].T.astype(F32), cells)
            stack = dot_nn(left, leaf_stack)
            folded[...] = stack.astype(BF16)
            left = expand(stack, cells)
            for j in range(GROUP):
                product[:, j * block:(j + 1) * block] = dot_nt(left, gath[pl.ds(j * block, block), :]).astype(BF16)

    def turn_spread():
        for part in range(2):
            for j in range(GROUP):
                turned = pnat[part, :, j * block:(j + 1) * block].T
                per = block // panel
                pt[part, pl.ds(j * per, per)] = turned.reshape(per, panel, cells)

    def order_spread(order):
        arrive("slots")
        for place, slot in enumerate(order):
            at = slots[0, slot]
            for part in range(2):
                pts[part, place * panel:(place + 1) * panel, :] = pt[part, at]

    by_z = range(GROUP * GROUP)
    by_r = [zz * GROUP + rr for rr in range(GROUP) for zz in range(GROUP)]

    def plain_end(values, at, peer):
        vall[at] = values.astype(BF16)
        gather_into(vall, at, peer, send_sem.at[0, 3], recv_sem.at[0, 3])
        wide = widen(jnp.concatenate([vall[k].astype(F32) for k in range(GROUP)], axis=1))
        forward = lead[0] - dot_nn(wide[:, :sep], pts[0]) - dot_nn(wide[:, sep:], pts[1])
        held[...] = forward
        fbuf[...] = forward.astype(BF16)
        send(fbuf, fone, one_send, one_recv, (ly + 1, me))

    def spread_out(s, values, own, sign, at, peer, to, whole):
        wide = widen(values)

        def pass_on(k):
            j = lax.rem(at + k, GROUP)
            if to is not None and not whole:
                send(obuf.at[s, j], frecv.at[k], y_send, y_recv, (to, peer(k)[1]))
            if k:
                send(obuf.at[s, j], orecv.at[s, k - 1], o_send.at[s], o_recv.at[s], peer(k))

        if whole:
            shares = sign * dot_nn(wide, po[...])
            for j in range(GROUP):
                prod[j] = shares[:, j * cells:(j + 1) * cells]
                obuf[s, j] = shares[:, j * cells:(j + 1) * cells].astype(BF16)
            total = own + prod[at]
            obuf[s, at] = total.astype(BF16)
            for k in ORDER + (0,):
                send(obuf.at[s], frow.at[k], y_send, w_recv, (to, peer(k)[1]))
            for k in ORDER:
                pass_on(k)
        else:
            for k in ORDER + (0,):
                j = lax.rem(at + k, GROUP)
                share = sign * dot_nn(wide, po[:, part_of(j, cells)])
                if not k:
                    share = total = own + share
                obuf[s, j] = share.astype(BF16)
                pass_on(k)
        wait_all(orecv.at[s], o_recv.at[s])
        for k in range(GROUP - 1):
            total = total + orecv[s, k].astype(F32)
        return total

    def own_cells():
        wait_all(frecv, y_recv)
        total = frecv[0].astype(F32)
        for k in range(1, GROUP):
            total = total + frecv[k].astype(F32)
        return widen(total)

    def group_cells():
        wait_all(frow, w_recv)
        wides = []
        for j in range(GROUP):
            total = frow[0, j].astype(F32)
            for k in range(1, GROUP):
                total = total + frow[k, j].astype(F32)
            prod[j] = total
            wides.append(widen(total))
        return jnp.concatenate(wides, axis=1)

    def columns(product, j):
        return product[:, part_of(j, block)]

    arrive_maps = ("below", "above", "spread")

    @pl.when(ly == 0)
    def _():
        scatter(0, r, row_peer, lambda j: const[j])
        for name in arrive_maps:
            arrive(name)
        turn_spread()
        order_spread(by_r)
        arrive("panel")
        for j in range(2 * GROUP):
            qown_t[j * block:(j + 1) * block, :] = qown[:, j * block:(j + 1) * block].T
        sums = add_up(0, 1, scattered(0, r), bbuf, brecv, col_peer)
        sall[r] = sums.astype(BF16)
        gather_into(sall, r, row_peer, send_sem.at[0, 2], recv_sem.at[0, 2])
        wide = widen(jnp.concatenate([sall[k].astype(F32) for k in range(GROUP)], axis=1))
        mine = dot_nn(wide, qown_t[...])
        vown[z] = jnp.concatenate([mine, jnp.zeros((ROWS, 128 - panel), F32)], axis=1).astype(BF16)
        gather_into(vown, z, col_peer, v_send, v_recv, lambda: fold(((below, lb_t, xb),)))
        share_product(xb, z, col_peer)
        share_inverse(z, col_peer)
        values = jnp.concatenate([vown[k].astype(F32)[:, :panel] for k in range(GROUP)], axis=1)
        plain_end(values, r, row_peer)
        share_spread(r, row_peer)
        take_spread()
        take_product()
        wide = group_cells()
        partial = dot_nn(wide, xo[...])
        held[...] = held[...] - dot_nn(widen(prod[z]), lb_t[...])
        values = values_of(1, partial, row_peer, col_peer, True)
        out[...] = spread_out(1, values, held[...], 1.0, r, row_peer, None, False)

    @pl.when(ly == 1)
    def _():
        share_inverse(r, row_peer)
        for name in arrive_maps:
            arrive(name)
        fold(((above, la_t, xa), (below, lb_t, xb)))
        turn_spread()
        order_spread(by_z)
        take_inverse()
        wait_all(fone, one_recv)
        wide = widen(fone[...].astype(F32))
        scatter(0, r, row_peer, lambda j: const[j] - dot_nn(wide, columns(xa, j)))
        lead[0] = lead[0] - dot_nn(wide, la_t[...])
        plain_end(values_of(0, scattered(0, r), col_peer, row_peer), z, col_peer)
        share_product(xb, r, row_peer)
        share_spread(z, col_peer)
        take_product()
        wide = group_cells()
        partial = dot_nn(wide, xo[...])
        held[...] = held[...] - dot_nn(widen(prod[r]), lb_t[...])
        values = values_of(1, partial, col_peer, row_peer)
        take_spread()
        out[...] = spread_out(1, values, held[...], 1.0, z, col_peer, 0, True)

    @pl.when(ly == 2)
    def _():
        share_inverse(z, col_peer)
        for name in arrive_maps:
            arrive(name)
        turn_spread()
        order_spread(by_r)
        share_spread(r, row_peer)
        fold(((above, la_t, xa), (below, lb_t, xb)))
        take_inverse()
        take_spread()
        wait_all(fone, one_recv)
        wide = widen(fone[...].astype(F32))
        scatter(0, z, col_peer, lambda j: const[j] - dot_nn(wide, columns(xa, j)))
        lead[0] = lead[0] - dot_nn(wide, la_t[...])
        values = values_of(0, scattered(0, z), row_peer, col_peer)
        held[...] = spread_out(0, values, lead[0], -1.0, r, row_peer, 3, True)
        wait_all(frow, y_send)
        wide = own_cells()
        scatter(1, z, col_peer, lambda j: dot_nn(wide, columns(xb, j)))
        held[...] = held[...] - dot_nn(wide, lb_t[...])
        values = values_of(1, scattered(1, z), row_peer, col_peer)
        out[...] = spread_out(1, values, held[...], 1.0, r, row_peer, 1, True)
        wait_all(frow, y_send)

    @pl.when(ly == 3)
    def _():
        share_inverse(r, row_peer)
        for k in ORDER:
            send(const.at[lax.rem(r + k, GROUP)], crow.at[k - 1], bulk_send.at[C_AT], bulk_recv.at[C_AT], row_peer(k))
        for name in arrive_maps:
            arrive(name)
        turn_spread()
        order_spread(by_z)
        share_spread(z, col_peer)
        fold(((above, la_t, xa),))
        share_product(xa, r, row_peer)
        wait_all(bulk[C_AT], bulk_recv.at[C_AT])
        known = const[r]
        for k in range(GROUP - 1):
            known = known + crow[k]
        crow[0] = known
        take_inverse()
        take_product()
        wide = group_cells()
        partial = crow[0] - dot_nn(wide, xo[...])
        lead[0] = lead[0] - dot_nn(widen(prod[r]), la_t[...])
        values = values_of(0, partial, col_peer, row_peer)
        take_spread()
        out[...] = spread_out(0, values, lead[0], -1.0, z, col_peer, 2, False)

    wait_all(bulk[Q_AT], bulk_send.at[Q_AT])
    wait_all(bulk[P_AT], bulk_send.at[P_AT])

    def left(s, phases):
        for phase in phases:
            wait_all((arecv, brecv, crecv)[phase].at[s], send_sem.at[s, phase])

    @pl.when(ly == 0)
    def _():
        left(0, (0, 1, 2))
        wait_all(vown.at[pl.ds(0, GROUP - 1)], v_send)
        wait_all(bulk[X_AT], bulk_send.at[X_AT])
        left(1, (1, 2))
        wait_all(orecv.at[1], o_send.at[1])

    @pl.when(ly == 1)
    def _():
        left(0, (0, 1, 2))
        left(1, (1, 2))
        wait_all(bulk[X_AT], bulk_send.at[X_AT])
        wait_all(frow, y_send)
        wait_all(orecv.at[1], o_send.at[1])

    @pl.when(ly < 2)
    def _():
        wait_all(vall.at[pl.ds(0, GROUP - 1)], send_sem.at[0, 3])
        wait_all(fone, one_send)

    @pl.when(ly == 2)
    def _():
        left(0, (0, 1, 2))
        left(1, (0, 1, 2))
        for s in range(2):
            wait_all(orecv.at[s], o_send.at[s])

    @pl.when(ly == 3)
    def _():
        left(0, (1, 2))
        wait_all(bulk[X_AT], bulk_send.at[X_AT])
        wait_all(bulk[C_AT], bulk_send.at[C_AT])
        wait_all(frecv, y_send)
        wait_all(orecv.at[0], o_send.at[0])


def local(right_sides, leaf, above, below, gather, inverse, spread, owner):
    depth = lax.axis_size("layer")
    _, _, count, cells = right_sides.shape
    panel, sep = inverse.shape[2], inverse.shape[3]
    block = sep // GROUP
    vmem = pl.BlockSpec(memory_space=pltpu.VMEM)
    hbm = pl.BlockSpec(memory_space=pl.ANY)
    dma = pltpu.SemaphoreType.DMA
    V = pltpu.VMEM
    out = pl.pallas_call(
        functools.partial(kernel, depth, cells, sep, panel),
        out_shape=pltpu.VMEM((ROWS, cells), F32),
        in_specs=[vmem, vmem] + [hbm] * 6,
        out_specs=vmem,
        scratch_shapes=[
            V((cells, 2 * cells), BF16),
            V((cells, 2 * cells), BF16),
            V((cells, 2 * cells), BF16),
            V((sep, 2 * cells), BF16),
            V((block, 2 * block), BF16),
            V((2, cells, sep), BF16),
            V((2 * cells, cells), BF16),
            V((2 * cells, cells), BF16),
            V((2 * cells, cells), BF16),
            V((2 * cells, sep), BF16),
            V((2 * cells, sep), BF16),
            V((GROUP * 2 * cells, block), BF16),
            V((2 * block, block), BF16),
            V((2, sep // panel, panel, cells), BF16),
            V((2, sep, cells), BF16),
            V((2 * block, GROUP * cells), BF16),
            V((panel, 2 * sep), BF16),
            V((2 * sep, panel), BF16),
            V((2, GROUP, ROWS, block), BF16),
            V((2, GROUP - 1, ROWS, block), BF16),
            V((2, ROWS, block), BF16),
            V((2, GROUP - 1, ROWS, block), BF16),
            V((2, ROWS, block), BF16),
            V((2, GROUP - 1, ROWS, block), BF16),
            V((GROUP - 1, ROWS, block), F32),
            V((GROUP, ROWS, block), BF16),
            V((GROUP, ROWS, 128), BF16),
            V((GROUP, ROWS, block), BF16),
            V((ROWS, cells), BF16),
            V((ROWS, cells), BF16),
            V((2, GROUP, ROWS, cells), BF16),
            V((2, GROUP - 1, ROWS, cells), BF16),
            V((GROUP, ROWS, cells), BF16),
            V((GROUP, GROUP, ROWS, cells), BF16),
            V((GROUP, ROWS, block), F32),
            V((1, ROWS, cells), F32),
            V((ROWS, cells), F32),
            V((GROUP, ROWS, cells), F32),
            V((1, 128), jnp.int32),
            pltpu.SMEM((1, 128), jnp.int32),
            dma((14,)),
            dma((2, 4)), dma((2, 4)),
            dma((4,)), dma((4,)),
            dma, dma,
            dma, dma, dma,
            dma((2,)), dma((2,)),
            dma, dma,
        ],
        compiler_params=pltpu.CompilerParams(
            collective_id=0, has_side_effects=True, vmem_limit_bytes=60 * 2**20),
        name="sweep",
    )(owner, right_sides.reshape(ROWS, cells), leaf[0], above[0], below[0], gather[0], inverse[0], spread[0])
    return out.reshape(1, 2, count, cells)


def solution(mesh):
    return jax.shard_map(
        local,
        mesh=mesh,
        in_specs=(
            P("layer", None, None, "front"),
            P("layer", None, "front", None),
            P("layer", None, "front", None),
            P("layer", None, "front", None),
            P("layer", None, None, "front"),
            P("layer", None, "front", None),
            P("layer", None, "front", None),
            P("layer", None),
        ),
        out_specs=P("layer", None, None, "front"),
        check_vma=False,
    )
```
